128 devices in a mesh: feed: 32 (over y_hi, x, z), tm: 4 (over y_lo, core).
Axes of the slice: x: 4, y: 4 (y_hi: 2, y_lo: 2; y = y_hi * 2 + y_lo), z: 4, core: 2. Of those that a mesh axis runs over, the one named last changes fastest.
Arguments:
- voltages: int32 [512, 524288], P('feed', 'tm'), may hold values from -128 to 127, as said below
- pfb_taps: float32 [16, 2048], replicated, may hold values from -3 to 3
- feed_flags: int32 [512], P('feed'), may hold values 0 or 1
Outputs:
- visibility: float32 [1024, 2, 512, 512], P(('feed', 'tm'))
The draws below stay inside these ranges and needn't reach their ends.
Inputs may be any that keep to these rules, and one draw needn't show every extreme that they name: `voltages`: signed 8-bit sample values.
All inputs are finite; a program needn't handle non-finite values. No bound on the sum of `feed_flags` on one device may be relied on, other than what follows from the above.
Results may differ from the reference program's by a relative error of at most 0.0019.
Values may be sent and summed in bfloat16 or wider, within the bound.
A program may use at most 128 MiB of HBM per device.

```python
import math
import jax
import jax.numpy as jnp
from jax import lax

INPUTS = 512
CH = 1024
TAPS = 16
FRAME = 2048
SPECTRA = 256
SAMPLES = 524288


def draw_voltages(key, part):
    common_key = jax.random.fold_in(key, 11)
    gain_key = jax.random.fold_in(key, 23)
    noise_key = jax.random.fold_in(key, 37)
    common = jax.random.randint(common_key, (1, SAMPLES), -48, 49)
    gain_steps = jax.random.randint(gain_key, (INPUTS, 1), -3, 4)
    noise_part = jax.random.randint(noise_key, (INPUTS, SAMPLES), -64, 65)
    return jnp.clip(gain_steps * common + noise_part, -128, 127).astype(jnp.int32)


def touch_ends(array, rng, low, largest):
    index_at = [jax.random.randint(jax.random.fold_in(rng, axis), (), 0, length) for axis, length in enumerate(array.shape)]
    main_axis = array.shape.index(max(array.shape))
    next_to = index_at[:main_axis] + [(index_at[main_axis] + 1) % array.shape[main_axis]] + index_at[main_axis + 1:]
    return array.at[tuple(index_at)].set(low).at[tuple(next_to)].set(largest)


def gaussian(own_key, extent, width, most, dtype=jnp.bfloat16):
    return jnp.clip(width * jax.random.normal(own_key, extent, jnp.float32), -most, most).astype(dtype)


def setup_inputs(seed: int = 0) -> dict:
    splits = jax.random.split(jax.random.key(seed), 4)
    voltages = draw_voltages(jax.random.fold_in(splits[3], 71), 0)
    pfb_taps = gaussian(splits[1], (TAPS, FRAME), 0.5, 3.0, jnp.float32)
    feed_flags = touch_ends((jax.random.randint(splits[2], (INPUTS,), 0, 8) < 7).astype(jnp.int32), jax.random.fold_in(splits[2], 1), 0, 1)
    return {"voltages": voltages, "pfb_taps": pfb_taps, "feed_flags": feed_flags}


def correlate(block):
    values = block.astype(jnp.float32)
    swapped = jnp.stack([values[:, 1], -values[:, 0]], axis=1)
    vis_real = jnp.einsum('cris,crjs->cij', values, values, precision=lax.Precision.HIGHEST)
    vis_imag = jnp.einsum('cris,crjs->cij', swapped, values, precision=lax.Precision.HIGHEST)
    return jnp.stack([vis_real, vis_imag], axis=1) / SPECTRA

def reference(voltages, pfb_taps, feed_flags):
    frames = (voltages.astype(jnp.float32) / 128.0).reshape(INPUTS, SPECTRA, FRAME)
    padded = jnp.concatenate([jnp.zeros((INPUTS, TAPS - 1, FRAME), jnp.float32), frames], axis=1)
    running = jnp.zeros((INPUTS, SPECTRA, FRAME), jnp.float32)
    for tap_lag in range(TAPS):
        offset = TAPS - 1 - tap_lag
        running = running + pfb_taps[tap_lag] * padded[:, offset:offset + SPECTRA, :]
    kept_mask = feed_flags.astype(jnp.float32)[:, None, None]
    filtered = (running * kept_mask).astype(jnp.bfloat16)
    spectrum = jnp.fft.rfft(filtered.astype(jnp.float32), axis=-1)[:, :, :CH] / math.sqrt(FRAME)
    real_part = jnp.real(spectrum).astype(jnp.bfloat16)
    imag_part = jnp.imag(spectrum).astype(jnp.bfloat16)
    stacked = jnp.stack([real_part, imag_part])
    block_len = min(64, CH)
    stacked = jnp.transpose(stacked, (3, 0, 1, 2)).reshape(CH // block_len, block_len, 2, INPUTS, SPECTRA)
    result = lax.map(correlate, stacked)
    return result.reshape(CH, 2, INPUTS, INPUTS)
```

```python
import functools
import math

import jax
import jax.numpy as jnp
import numpy as np
from jax import lax
from jax.experimental import pallas as pl
from jax.experimental.pallas import tpu as pltpu
from jax.sharding import PartitionSpec as P

MESH = pl.DeviceIdType.MESH
LANES = 128
FRAME = 2048
HALF = FRAME // 2
TAPS = 16
FEEDS, TIMES = 32, 4
DEVICES = FEEDS * TIMES
SPEC = 64
OCT = 8
BLOCKS = SPEC // 16


def link_loads(offset):
    loads = [0] * 6
    for axis, step in enumerate(offset[1:]):
        if step in (1, 2):
            loads[2 * axis] += 1
        if step in (2, 3):
            loads[2 * axis + 1] += 1
    return loads


def send_order():
    left = [
        (c, y, x, z)
        for z in range(4)
        for x in range(4)
        for y in range(4)
        for c in range(2)
        if (c, y, x, z) != (0, 0, 0, 0)
    ]
    mixed = [left[(37 * i + 11) % len(left)] for i in range(len(left))]
    order, total = [], [0] * 6
    while mixed:
        def spread(offset):
            sums = [a + b for a, b in zip(total, link_loads(offset))]
            mean = sum(sums) / 6
            return sum((s - mean) ** 2 for s in sums)

        best = min(mixed, key=spread)
        mixed.remove(best)
        order.append(best)
        total = [a + b for a, b in zip(total, link_loads(best))]
    return order


ORDER = send_order()


def peer(offset, feed, time):
    dc, dy, dx, dz = offset
    y = feed // 16 * 2 + time // 2
    x = lax.rem(feed // 4 % 4 + dx, 4)
    z = lax.rem(feed % 4 + dz, 4)
    y = lax.rem(y + dy, 4)
    c = lax.rem(time % 2 + dc, 2)
    return y // 2 * 16 + x * 4 + z, y % 2 * 2 + c


def phase_tables():
    n = np.arange(HALF)
    coarse = np.exp(-2j * np.pi * ((16 * np.arange(64)[:, None] * n) % FRAME) / FRAME)
    rows = 8 * np.arange(2)[:, None] + 2 * np.arange(4)
    rows = rows.reshape(8)[None, :, None] + np.arange(2)[:, None, None]
    scale = 1.0 / (128 * 16 * math.sqrt(FRAME))
    fine = scale * np.exp(-2j * np.pi * (rows * n % FRAME) / FRAME)
    coarse = np.stack([coarse.real, coarse.imag]).astype(np.float32)
    fine = np.stack([fine.real, fine.imag], axis=1).astype(np.float32)
    return coarse, fine


def channelise(
    volt_hbm, taps_ref, flag_ref, coarse_ref, fine_ref, out_ref,
    volt, edge, halo, table_hi, table_lo, folded, spectra, packed,
    in_sem, halo_send, halo_recv, send_sem, recv_sem, own_sem,
):
    feed, time = lax.axis_index("feed"), lax.axis_index("tm")
    me = feed * TIMES + time

    tail = (SPEC - 16) * FRAME
    loads = []
    for o in range(2):
        loads.append(pltpu.make_async_copy(
            volt_hbm.at[pl.ds(o * OCT, OCT), pl.ds(tail, 16 * FRAME)],
            volt.at[o, :, pl.ds(tail, 16 * FRAME)], in_sem.at[o, 0]))
    for o in range(2):
        loads.append(pltpu.make_async_copy(
            volt_hbm.at[pl.ds(o * OCT, OCT), pl.ds(0, tail)],
            volt.at[o, :, pl.ds(0, tail)], in_sem.at[o, 1]))
    for load in loads:
        load.start()

    barrier = pltpu.get_barrier_semaphore()

    def greet(step, carry):
        other = lax.rem(me + step, DEVICES)
        pl.semaphore_signal(barrier, inc=1, device_id=(other // TIMES, other % TIMES), device_id_type=MESH)
        return carry

    lax.fori_loop(1, DEVICES, greet, 0)

    def make_table(q):
        fine_re, fine_im = fine_ref[q, 0], fine_ref[q, 1]

        def rows(pair, carry):
            parts = []
            for side in range(2):
                a_re = coarse_ref[0, pl.ds(pair * 2 + side, 1), :]
                a_im = coarse_ref[1, pl.ds(pair * 2 + side, 1), :]
                parts.append((a_re * fine_re - a_im * fine_im, a_re * fine_im + a_im * fine_re))
            for c in range(2):
                value = jnp.concatenate([parts[0][c], parts[1][c]], axis=0)
                high = value.astype(jnp.bfloat16)
                low = (value - high.astype(jnp.float32)).astype(jnp.bfloat16)
                at = pl.ds(pl.multiple_of(pair * 16, 16), 16)
                table_hi[q, c, at, :] = high
                table_lo[q, c, at, :] = low
            return carry

        lax.fori_loop(0, 32, rows, 0)

    make_table(0)

    for o in range(2):
        loads[o].wait()

        def pack_edge(nb, carry, o=o):
            for pair in range(8):
                two = []
                for side in range(2):
                    at = pl.multiple_of(tail + (pair * 2 + side) * FRAME + nb * LANES, LANES)
                    two.append(volt[o, :, pl.ds(at, LANES)].astype(jnp.float32))
                lanes = pl.ds(pl.multiple_of(nb * LANES, LANES), LANES)
                edge[o, pair, :, lanes] = jnp.concatenate(two, axis=0).astype(jnp.bfloat16)
            return carry

        lax.fori_loop(0, FRAME // LANES, pack_edge, 0)

    pl.semaphore_wait(barrier, DEVICES - 1)

    def halo_copy(o):
        return pltpu.make_async_remote_copy(
            src_ref=edge.at[o], dst_ref=halo.at[o], send_sem=halo_send.at[o], recv_sem=halo_recv.at[o],
            device_id=(feed, lax.rem(time + 1, TIMES)), device_id_type=MESH)

    @pl.when(time < TIMES - 1)
    def _():
        for o in range(2):
            halo_copy(o).start()

    @pl.when(time == 0)
    def _():
        halo[...] = jnp.zeros_like(halo)

    def filter_block(o, mb, nb, first):
        flag = flag_ref[o]
        sides = []
        for side in range(2):
            lane0 = nb * LANES + side * HALF
            lanes = pl.ds(pl.multiple_of(lane0, LANES), LANES)
            taps = [jnp.broadcast_to(taps_ref[pl.ds(p, 1), lanes], (OCT, LANES)) for p in range(TAPS)]
            sums = [None] * 16
            early = None
            for j in range(-15, 16):
                if first and j < 0:
                    pair, odd = (16 + j) // 2, (16 + j) % 2
                    if odd == 0 or early is None:
                        early = halo[o, pair, :, lanes].astype(jnp.float32)
                    x = early[odd * OCT:(odd + 1) * OCT]
                else:
                    at = pl.multiple_of((mb * 16 + j) * FRAME + lane0, LANES)
                    x = volt[o, :, pl.ds(at, LANES)].astype(jnp.float32)
                for m in range(max(0, j), min(15, j + 15) + 1):
                    term = taps[m - j] * x
                    sums[m] = term if sums[m] is None else sums[m] + term
            value = jnp.stack([s * flag for s in sums])
            value = jnp.swapaxes(value, 0, 1)
            sides.append(value.astype(jnp.bfloat16).astype(jnp.float32))
        rows = pl.ds(pl.multiple_of(mb * 16, 16), 16)
        lanes = pl.ds(pl.multiple_of(nb * LANES, LANES), LANES)
        folded[o, 0, :, rows, lanes] = (sides[0] + sides[1]).astype(jnp.bfloat16)
        folded[o, 1, :, rows, lanes] = (sides[0] - sides[1]).astype(jnp.bfloat16)

    for o in range(2):
        loads[2 + o].wait()

    def later_blocks(step, carry):
        o = step // (8 * (BLOCKS - 1))
        rest = step % (8 * (BLOCKS - 1))
        filter_block(o, 1 + rest // 8, rest % 8, False)
        return carry

    lax.fori_loop(0, 2 * 8 * (BLOCKS - 1), later_blocks, 0)

    lane = lax.broadcasted_iota(jnp.int32, (8, LANES), 1)
    left_half = lane < SPEC

    def exchange(o, q, other_feed, other_time):
        return pltpu.make_async_remote_copy(
            src_ref=packed.at[other_feed * TIMES + other_time, o, q],
            dst_ref=out_ref.at[q, pl.ds(0, 2), time, feed, o],
            send_sem=send_sem, recv_sem=recv_sem, device_id=(other_feed, other_time), device_id_type=MESH)

    def own_copy(o, q):
        return pltpu.make_async_copy(
            packed.at[me, o, q], out_ref.at[q, pl.ds(0, 2), time, feed, o], own_sem)

    def octet(o, carry):
        @pl.when(time > 0)
        def _():
            halo_copy(o).wait_recv()

        def first_block(nb, c):
            filter_block(o, 0, nb, True)
            return c

        lax.fori_loop(0, 8, first_block, 0)

        def parity(q, carry):
            @pl.when((o == 0) & (q == 1))
            def _():
                make_table(1)

            right = folded[o, q].reshape(OCT * SPEC, HALF)
            dims = (((1,), (1,)), ((), ()))
            for c in range(2):
                spectra[c] = lax.dot_general(
                    table_hi[q, c], right, dims, preferred_element_type=jnp.float32
                ) + lax.dot_general(table_lo[q, c], right, dims, preferred_element_type=jnp.float32)

            def turn(g, c):
                rows = pl.ds(pl.multiple_of(g * 8, 8), 8)
                tiles = []
                for pair in range(OCT // 2):
                    re = spectra[0, rows, pair * LANES:(pair + 1) * LANES]
                    im = spectra[1, rows, pair * LANES:(pair + 1) * LANES]
                    tiles.append(jnp.where(left_half, re, pltpu.roll(im, SPEC, 1)))
                    tiles.append(jnp.where(left_half, pltpu.roll(re, SPEC, 1), im))
                tile = jnp.swapaxes(jnp.stack(tiles), 0, 1)
                packed[pl.ds(g * 2, 2), o, q] = tile.reshape(2, 2, 16, LANES).astype(jnp.bfloat16)
                return c

            lax.fori_loop(0, DEVICES // 2, turn, 0)
            for offset in ORDER:
                exchange(o, q, *peer(offset, feed, time)).start()
            own_copy(o, q).start()
            return carry

        lax.fori_loop(0, 2, parity, 0)
        return carry

    lax.fori_loop(0, 2, octet, 0)

    @pl.when(time < TIMES - 1)
    def _():
        for o in range(2):
            halo_copy(o).wait_send()

    everything = pltpu.make_async_remote_copy(
        src_ref=packed.at[pl.ds(0, DEVICES - 1)], dst_ref=packed.at[pl.ds(0, DEVICES - 1)],
        send_sem=send_sem, recv_sem=recv_sem, device_id=(feed, time), device_id_type=MESH)
    everything.wait()
    own = packed.at[0]
    pltpu.make_async_copy(own, own, own_sem).wait()


def gather_spectra(voltages, pfb_taps, flags, coarse, fine):
    vmem = pl.BlockSpec(memory_space=pltpu.VMEM)
    return pl.pallas_call(
        channelise,
        out_shape=jax.ShapeDtypeStruct((2, 2, TIMES, FEEDS, 2, 16, LANES), jnp.bfloat16),
        in_specs=[pl.BlockSpec(memory_space=pl.ANY), vmem, vmem, vmem, vmem],
        out_specs=pl.BlockSpec(memory_space=pl.ANY),
        scratch_shapes=[
            pltpu.VMEM((2, OCT, SPEC * FRAME), jnp.int32),
            pltpu.VMEM((2, 8, 16, FRAME), jnp.bfloat16),
            pltpu.VMEM((2, 8, 16, FRAME), jnp.bfloat16),
            pltpu.VMEM((2, 2, 512, HALF), jnp.bfloat16),
            pltpu.VMEM((2, 2, 512, HALF), jnp.bfloat16),
            pltpu.VMEM((2, 2, OCT, SPEC, HALF), jnp.bfloat16),
            pltpu.VMEM((2, 512, OCT * SPEC), jnp.float32),
            pltpu.VMEM((DEVICES, 2, 2, 2, 16, LANES), jnp.bfloat16),
            pltpu.SemaphoreType.DMA((2, 2)),
            pltpu.SemaphoreType.DMA((2,)),
            pltpu.SemaphoreType.DMA((2,)),
            pltpu.SemaphoreType.DMA,
            pltpu.SemaphoreType.DMA,
            pltpu.SemaphoreType.DMA,
        ],
        compiler_params=pltpu.CompilerParams(
            collective_id=0, has_side_effects=True, vmem_limit_bytes=48 << 20),
        name="channelise",
    )(voltages, pfb_taps, flags, coarse, fine)


def correlate(block_ref, out_ref, left, right):
    which = pl.program_id(2)
    lane = lax.broadcasted_iota(jnp.int32, (8, LANES), 1)

    for other in range(2):
        @pl.when(which == other)
        def _():
            for t in range(TIMES):
                tile = block_ref[0, 0, t].astype(jnp.float32)
                tile = tile[:, :, other * OCT:(other + 1) * OCT, :].reshape(512, LANES)
                cols = slice(t * LANES, (t + 1) * LANES)
                right[:, cols] = tile.astype(jnp.bfloat16)
                sign = jnp.where(lane[:1] < SPEC, 1.0, -1.0)
                left[:, cols] = (pltpu.roll(tile, SPEC, 1) * sign).astype(jnp.bfloat16)

    dims = (((1,), (1,)), ((), ()))
    value = right[...]
    out_ref[0, 0, 0, 0] = lax.dot_general(value, value, dims, preferred_element_type=jnp.float32)
    out_ref[0, 0, 0, 1] = lax.dot_general(left[...], value, dims, preferred_element_type=jnp.float32)


def visibilities(gathered):
    out = pl.pallas_call(
        correlate,
        out_shape=jax.ShapeDtypeStruct((2, 2, 2, 2, 512, 512), jnp.float32),
        grid=(2, 2, 2),
        in_specs=[pl.BlockSpec((1, 1, TIMES, FEEDS, 2, 16, LANES), lambda q, p, j: (q, p, 0, 0, 0, 0, 0))],
        out_specs=pl.BlockSpec((1, 1, 1, 2, 512, 512), lambda q, p, j: (p, j, q, 0, 0, 0)),
        scratch_shapes=[pltpu.VMEM((512, 512), jnp.bfloat16), pltpu.VMEM((512, 512), jnp.bfloat16)],
        compiler_params=pltpu.CompilerParams(vmem_limit_bytes=32 << 20),
        name="correlate",
    )(gathered)
    return out.reshape(8, 2, 512, 512)


def per_device(voltages, pfb_taps, feed_flags):
    coarse, fine = phase_tables()
    flags = jnp.broadcast_to(feed_flags.astype(jnp.float32).reshape(2, OCT, 1), (2, OCT, LANES))
    return visibilities(gather_spectra(voltages, pfb_taps, flags, jnp.asarray(coarse), jnp.asarray(fine)))


def solution(mesh):
    return jax.shard_map(
        per_device,
        mesh=mesh,
        in_specs=(P("feed", "tm"), P(), P("feed")),
        out_specs=P(("feed", "tm"), None, None, None),
        check_vma=False,
    )
```

```python
import functools
import math

import jax
import jax.numpy as jnp
import numpy as np
from jax import lax
from jax.experimental import pallas as pl
from jax.experimental.pallas import tpu as pltpu
from jax.sharding import PartitionSpec as P

MESH = pl.DeviceIdType.MESH
LANES = 128
FRAME = 2048
HALF = FRAME // 2
TAPS = 16
FEEDS, TIMES = 32, 4
DEVICES = FEEDS * TIMES
SPEC = 64
OCT = 8
BLOCKS = SPEC // 16


def link_loads(offset):
    loads = [0] * 6
    for axis, step in enumerate(offset[1:]):
        if step in (1, 2):
            loads[2 * axis] += 1
        if step in (2, 3):
            loads[2 * axis + 1] += 1
    return loads


def send_order():
    left = [
        (c, y, x, z)
        for z in range(4)
        for x in range(4)
        for y in range(4)
        for c in range(2)
        if (c, y, x, z) != (0, 0, 0, 0)
    ]
    mixed = [left[(37 * i + 11) % len(left)] for i in range(len(left))]
    order, total = [], [0] * 6
    while mixed:
        def spread(offset):
            sums = [a + b for a, b in zip(total, link_loads(offset))]
            mean = sum(sums) / 6
            return sum((s - mean) ** 2 for s in sums)

        best = min(mixed, key=spread)
        mixed.remove(best)
        order.append(best)
        total = [a + b for a, b in zip(total, link_loads(best))]
    return order


ORDER = send_order()


def peer(offset, feed, time):
    dc, dy, dx, dz = offset
    y = feed // 16 * 2 + time // 2
    x = lax.rem(feed // 4 % 4 + dx, 4)
    z = lax.rem(feed % 4 + dz, 4)
    y = lax.rem(y + dy, 4)
    c = lax.rem(time % 2 + dc, 2)
    return y // 2 * 16 + x * 4 + z, y % 2 * 2 + c


def phase_tables():
    n = np.arange(HALF)
    coarse = np.exp(-2j * np.pi * ((16 * np.arange(64)[:, None] * n) % FRAME) / FRAME)
    rows = 8 * np.arange(2)[:, None] + 2 * np.arange(4)
    rows = rows.reshape(8)[None, :, None] + np.arange(2)[:, None, None]
    scale = 1.0 / (128 * 16 * math.sqrt(FRAME))
    fine = scale * np.exp(-2j * np.pi * (rows * n % FRAME) / FRAME)
    coarse = np.stack([coarse.real, coarse.imag]).astype(np.float32)
    fine = np.stack([fine.real, fine.imag], axis=1).astype(np.float32)
    return coarse, fine


def channelise(
    volt_hbm, taps_hbm, flag_ref, coarse_hbm, fine_hbm, out_ref,
    volt, taps_ref, coarse_ref, fine_ref, edge, halo, table_hi, table_lo, folded, spectra, packed,
    in_sem, const_sem, halo_send, halo_recv, send_sem, recv_sem, own_sem,
):
    feed, time = lax.axis_index("feed"), lax.axis_index("tm")
    me = feed * TIMES + time

    tail = (SPEC - 16) * FRAME
    edges, bodies = [], []
    for o in range(2):
        inputs = pl.ds(o * OCT, OCT)
        edges.append(pltpu.make_async_copy(
            volt_hbm.at[inputs, pl.ds(tail, 16 * FRAME)], volt.at[o, :, pl.ds(tail, 16 * FRAME)], in_sem.at[o, 0]))
        bodies.append(pltpu.make_async_copy(
            volt_hbm.at[inputs, pl.ds(0, tail)], volt.at[o, :, pl.ds(0, tail)], in_sem.at[o, 1]))
    fine_load = pltpu.make_async_copy(fine_hbm, fine_ref, const_sem.at[0])
    coarse_load = pltpu.make_async_copy(coarse_hbm, coarse_ref, const_sem.at[1])
    taps_load = pltpu.make_async_copy(taps_hbm, taps_ref, const_sem.at[2])
    for load in (*edges, fine_load, coarse_load, taps_load, *bodies):
        load.start()

    barrier = pltpu.get_barrier_semaphore()

    def greet(step, carry):
        other = lax.rem(me + step, DEVICES)
        pl.semaphore_signal(barrier, inc=1, device_id=(other // TIMES, other % TIMES), device_id_type=MESH)
        return carry

    lax.fori_loop(1, DEVICES, greet, 0)

    def make_table(q):
        fine_re, fine_im = fine_ref[q, 0], fine_ref[q, 1]

        def rows(pair, carry):
            parts = []
            for side in range(2):
                a_re = coarse_ref[0, pl.ds(pair * 2 + side, 1), :]
                a_im = coarse_ref[1, pl.ds(pair * 2 + side, 1), :]
                parts.append((a_re * fine_re - a_im * fine_im, a_re * fine_im + a_im * fine_re))
            for c in range(2):
                value = jnp.concatenate([parts[0][c], parts[1][c]], axis=0)
                high = value.astype(jnp.bfloat16)
                low = (value - high.astype(jnp.float32)).astype(jnp.bfloat16)
                at = pl.ds(pl.multiple_of(pair * 16, 16), 16)
                table_hi[q, c, at, :] = high
                table_lo[q, c, at, :] = low
            return carry

        lax.fori_loop(0, 32, rows, 0)

    for o in range(2):
        edges[o].wait()

    @pl.when(time < TIMES - 1)
    def _():
        def pack_edge(nb, carry):
            lanes = pl.ds(pl.multiple_of(nb * LANES, LANES), LANES)
            for o in range(2):
                for pair in range(8):
                    two = []
                    for side in range(2):
                        at = pl.multiple_of(tail + (pair * 2 + side) * FRAME + nb * LANES, LANES)
                        two.append(volt[o, :, pl.ds(at, LANES)].astype(jnp.float32))
                    edge[o, pair, :, lanes] = jnp.concatenate(two, axis=0).astype(jnp.bfloat16)
            return carry

        lax.fori_loop(0, FRAME // LANES, pack_edge, 0)

    fine_load.wait()
    coarse_load.wait()
    make_table(0)

    pl.semaphore_wait(barrier, DEVICES - 1)

    def halo_copy(o):
        return pltpu.make_async_remote_copy(
            src_ref=edge.at[o], dst_ref=halo.at[o], send_sem=halo_send.at[o], recv_sem=halo_recv.at[o],
            device_id=(feed, lax.rem(time + 1, TIMES)), device_id_type=MESH)

    @pl.when(time < TIMES - 1)
    def _():
        for o in range(2):
            halo_copy(o).start()

    @pl.when(time == 0)
    def _():
        halo[...] = jnp.zeros_like(halo)

    taps_load.wait()
    sublane = lax.broadcasted_iota(jnp.int32, (OCT, LANES), 0)

    def flags_of(o):
        flag = jnp.zeros((OCT, LANES), jnp.float32)
        for i in range(OCT):
            flag = jnp.where(sublane == i, flag_ref[o * OCT + i].astype(jnp.float32), flag)
        return flag

    def filter_blocks(o, nb, flag, blocks):
        for mb in blocks:
            sides = []
            for side in range(2):
                lane0 = nb * LANES + side * HALF
                lanes = pl.ds(pl.multiple_of(lane0, LANES), LANES)
                taps = [jnp.broadcast_to(taps_ref[pl.ds(p, 1), lanes], (OCT, LANES)) for p in range(TAPS)]
                sums = [None] * 16
                early = None
                for j in range(-15, 16):
                    if mb == 0 and j < 0:
                        pair, odd = (16 + j) // 2, (16 + j) % 2
                        if odd == 0 or early is None:
                            early = halo[o, pair, :, lanes].astype(jnp.float32)
                        x = early[odd * OCT:(odd + 1) * OCT]
                    else:
                        at = pl.multiple_of((mb * 16 + j) * FRAME + lane0, LANES)
                        x = volt[o, :, pl.ds(at, LANES)].astype(jnp.float32)
                    for m in range(max(0, j), min(15, j + 15) + 1):
                        term = taps[m - j] * x
                        sums[m] = term if sums[m] is None else sums[m] + term
                value = jnp.swapaxes(jnp.stack([s * flag for s in sums]), 0, 1)
                sides.append(value.astype(jnp.bfloat16).astype(jnp.float32))
            rows = slice(mb * 16, (mb + 1) * 16)
            lanes = pl.ds(pl.multiple_of(nb * LANES, LANES), LANES)
            folded[o, 0, :, rows, lanes] = (sides[0] + sides[1]).astype(jnp.bfloat16)
            folded[o, 1, :, rows, lanes] = (sides[0] - sides[1]).astype(jnp.bfloat16)

    lane = lax.broadcasted_iota(jnp.int32, (8, LANES), 1)
    left_half = lane < SPEC

    def exchange(o, q, other_feed, other_time):
        return pltpu.make_async_remote_copy(
            src_ref=packed.at[other_feed * TIMES + other_time, o, q],
            dst_ref=out_ref.at[q, pl.ds(0, 2), time, feed, o],
            send_sem=send_sem, recv_sem=recv_sem, device_id=(other_feed, other_time), device_id_type=MESH)

    def own_copy(o, q):
        return pltpu.make_async_copy(
            packed.at[me, o, q], out_ref.at[q, pl.ds(0, 2), time, feed, o], own_sem)

    def octet(o, carry):
        flag = flags_of(o)

        def later_blocks(nb, c):
            filter_blocks(o, nb, flag, range(1, BLOCKS))
            return c

        def first_block(nb, c):
            filter_blocks(o, nb, flag, range(1))
            return c

        pltpu.make_async_copy(
            volt_hbm.at[pl.ds(0, OCT), pl.ds(0, tail)], volt.at[o, :, pl.ds(0, tail)], in_sem.at[o, 1]).wait()
        lax.fori_loop(0, 8, later_blocks, 0)

        @pl.when(time > 0)
        def _():
            halo_copy(o).wait_recv()

        lax.fori_loop(0, 8, first_block, 0)

        def parity(q, carry):
            @pl.when((o == 0) & (q == 1))
            def _():
                make_table(1)

            right = folded[o, q].reshape(OCT * SPEC, HALF)
            dims = (((1,), (1,)), ((), ()))
            for c in range(2):
                spectra[c] = lax.dot_general(
                    table_hi[q, c], right, dims, preferred_element_type=jnp.float32
                ) + lax.dot_general(table_lo[q, c], right, dims, preferred_element_type=jnp.float32)

            def turn(g, c):
                rows = pl.ds(pl.multiple_of(g * 8, 8), 8)
                tiles = []
                for pair in range(OCT // 2):
                    re = spectra[0, rows, pair * LANES:(pair + 1) * LANES]
                    im = spectra[1, rows, pair * LANES:(pair + 1) * LANES]
                    tiles.append(jnp.where(left_half, re, pltpu.roll(im, SPEC, 1)))
                    tiles.append(jnp.where(left_half, pltpu.roll(re, SPEC, 1), im))
                tile = jnp.swapaxes(jnp.stack(tiles), 0, 1)
                packed[pl.ds(g * 2, 2), o, q] = tile.reshape(2, 2, 16, LANES).astype(jnp.bfloat16)
                return c

            lax.fori_loop(0, DEVICES // 2, turn, 0, unroll=4)
            for offset in ORDER:
                exchange(o, q, *peer(offset, feed, time)).start()
            own_copy(o, q).start()
            return carry

        lax.fori_loop(0, 2, parity, 0)
        return carry

    lax.fori_loop(0, 2, octet, 0)

    @pl.when(time < TIMES - 1)
    def _():
        for o in range(2):
            halo_copy(o).wait_send()

    everything = pltpu.make_async_remote_copy(
        src_ref=packed.at[pl.ds(0, DEVICES - 1)], dst_ref=packed.at[pl.ds(0, DEVICES - 1)],
        send_sem=send_sem, recv_sem=recv_sem, device_id=(feed, time), device_id_type=MESH)
    everything.wait()
    own = packed.at[0]
    pltpu.make_async_copy(own, own, own_sem).wait()


def gather_spectra(voltages, pfb_taps, flags, coarse, fine):
    hbm = pl.BlockSpec(memory_space=pltpu.HBM)
    return pl.pallas_call(
        channelise,
        out_shape=jax.ShapeDtypeStruct((2, 2, TIMES, FEEDS, 2, 16, LANES), jnp.bfloat16),
        in_specs=[hbm, hbm, pl.BlockSpec(memory_space=pltpu.SMEM), hbm, hbm],
        out_specs=pl.BlockSpec(memory_space=pl.ANY),
        scratch_shapes=[
            pltpu.VMEM((2, OCT, SPEC * FRAME), jnp.int32),
            pltpu.VMEM((TAPS, FRAME), jnp.float32),
            pltpu.VMEM((2, 64, HALF), jnp.float32),
            pltpu.VMEM((2, 2, 8, HALF), jnp.float32),
            pltpu.VMEM((2, 8, 16, FRAME), jnp.bfloat16),
            pltpu.VMEM((2, 8, 16, FRAME), jnp.bfloat16),
            pltpu.VMEM((2, 2, 512, HALF), jnp.bfloat16),
            pltpu.VMEM((2, 2, 512, HALF), jnp.bfloat16),
            pltpu.VMEM((2, 2, OCT, SPEC, HALF), jnp.bfloat16),
            pltpu.VMEM((2, 512, OCT * SPEC), jnp.float32),
            pltpu.VMEM((DEVICES, 2, 2, 2, 16, LANES), jnp.bfloat16),
            pltpu.SemaphoreType.DMA((2, 2)),
            pltpu.SemaphoreType.DMA((3,)),
            pltpu.SemaphoreType.DMA((2,)),
            pltpu.SemaphoreType.DMA((2,)),
            pltpu.SemaphoreType.DMA,
            pltpu.SemaphoreType.DMA,
            pltpu.SemaphoreType.DMA,
        ],
        compiler_params=pltpu.CompilerParams(
            collective_id=0, has_side_effects=True, vmem_limit_bytes=48 << 20),
        name="channelise",
    )(voltages, pfb_taps, flags, coarse, fine)


def correlate(spec, out_hbm, left, right, result, out_sem):
    lane = lax.broadcasted_iota(jnp.int32, (1, LANES), 1)
    sign = jnp.where(lane < SPEC, 1.0, -1.0)
    dims = (((1,), (1,)), ((), ()))

    def put(step, j, c):
        q, p = step // 2, step % 2
        slot = step * 4 + j * 2 + c
        return pltpu.make_async_copy(result.at[slot], out_hbm.at[p, j, q, c], out_sem.at[slot])

    def channels(step, carry):
        q, p = step // 2, step % 2
        for j in range(2):
            for t in range(TIMES):
                tile = spec[q, p, t].astype(jnp.float32)
                tile = tile[:, :, j * OCT:(j + 1) * OCT, :].reshape(512, LANES)
                cols = slice(t * LANES, (t + 1) * LANES)
                right[j, :, cols] = tile.astype(jnp.bfloat16)
                left[j, :, cols] = (pltpu.roll(tile, SPEC, 1) * sign).astype(jnp.bfloat16)
            value = right[j]
            result[step * 4 + j * 2] = lax.dot_general(value, value, dims, preferred_element_type=jnp.float32)
            put(step, j, 0).start()
            result[step * 4 + j * 2 + 1] = lax.dot_general(left[j], value, dims, preferred_element_type=jnp.float32)
            put(step, j, 1).start()
        return carry

    lax.fori_loop(0, 4, channels, 0)
    for step in range(4):
        for j in range(2):
            for c in range(2):
                put(step, j, c).wait()


def visibilities(gathered):
    out = pl.pallas_call(
        correlate,
        out_shape=jax.ShapeDtypeStruct((2, 2, 2, 2, 512, 512), jnp.float32),
        in_specs=[pl.BlockSpec(memory_space=pltpu.VMEM)],
        out_specs=pl.BlockSpec(memory_space=pltpu.HBM),
        scratch_shapes=[
            pltpu.VMEM((2, 512, 512), jnp.bfloat16),
            pltpu.VMEM((2, 512, 512), jnp.bfloat16),
            pltpu.VMEM((16, 512, 512), jnp.float32),
            pltpu.SemaphoreType.DMA((16,)),
        ],
        compiler_params=pltpu.CompilerParams(vmem_limit_bytes=48 << 20),
        name="correlate",
    )(gathered)
    return out.reshape(8, 2, 512, 512)


def per_device(voltages, pfb_taps, feed_flags):
    coarse, fine = phase_tables()
    pinned = [
        pltpu.with_memory_space_constraint(x, pltpu.HBM)
        for x in (voltages, pfb_taps, feed_flags, jnp.asarray(coarse), jnp.asarray(fine))
    ]
    return visibilities(gather_spectra(*pinned))


def solution(mesh):
    return jax.shard_map(
        per_device,
        mesh=mesh,
        in_specs=(P("feed", "tm"), P(), P("feed")),
        out_specs=P(("feed", "tm"), None, None, None),
        check_vma=False,
    )
```

```python
import functools
import math

import jax
import jax.numpy as jnp
import numpy as np
from jax import lax
from jax.experimental import pallas as pl
from jax.experimental.pallas import tpu as pltpu
from jax.sharding import PartitionSpec as P

MESH = pl.DeviceIdType.MESH
LANES = 128
FRAME = 2048
HALF = FRAME // 2
TAPS = 16
FEEDS, TIMES = 32, 4
DEVICES = FEEDS * TIMES
SPEC = 64
OCT = 8
BLOCKS = SPEC // 16


def peers(section, feed, time):
    core, y, x, z = time % 2, feed // 16 * 2 + time // 2, feed // 4 % 4, feed % 4
    cores = [lax.rem(core + i, 2) for i in range(2)]
    ys = [lax.rem(y + i, 4) for i in range(4)]
    ys = [(lax.div(v, 2) * 16, lax.rem(v, 2) * 2) for v in ys]
    xs = [lax.rem(x + i, 4) * 4 for i in range(4)]
    zs = [lax.rem(z + i + 3 * section, 4) for i in range(4)]
    found = []
    for i in range(32):
        offset = i * 47 % DEVICES
        y_feed, y_time = ys[offset // 2 % 4]
        found.append((y_feed + xs[offset // 8 % 4] + zs[offset // 32], y_time + cores[offset % 2]))
    return found


def phase_tables():
    n = np.arange(HALF)
    coarse = np.exp(-2j * np.pi * ((8 * np.arange(DEVICES)[:, None] * n) % FRAME) / FRAME)
    rows = np.tile(2 * np.arange(4), 2)[None, :, None] + np.arange(2)[:, None, None]
    scale = 1.0 / (128 * 16 * math.sqrt(FRAME))
    fine = scale * np.exp(-2j * np.pi * (rows * n % FRAME) / FRAME)
    coarse = np.stack([coarse.real, coarse.imag]).astype(np.float32)
    fine = np.stack([fine.real, fine.imag], axis=1).astype(np.float32)
    return coarse, fine


def channelise(
    volt_hbm, taps_hbm, flag_ref, coarse_hbm, fine_hbm, out_ref,
    volt, taps_ref, coarse_ref, fine_ref, edge, halo, table, folded, spectra, packed,
    in_sem, const_sem, halo_send, halo_recv, send_sem, recv_sem, own_sem,
):
    feed, time = lax.axis_index("feed"), lax.axis_index("tm")

    tail = (SPEC - 16) * FRAME
    edges, bodies = [], []
    for o in range(2):
        inputs = pl.ds(o * OCT, OCT)
        edges.append(pltpu.make_async_copy(
            volt_hbm.at[inputs, pl.ds(tail, 16 * FRAME)], volt.at[o, :, pl.ds(tail, 16 * FRAME)], in_sem.at[o, 0]))
        bodies.append(pltpu.make_async_copy(
            volt_hbm.at[inputs, pl.ds(0, tail)], volt.at[o, :, pl.ds(0, tail)], in_sem.at[o, 1]))
    fine_load = pltpu.make_async_copy(fine_hbm, fine_ref, const_sem.at[0])
    coarse_load = pltpu.make_async_copy(coarse_hbm, coarse_ref, const_sem.at[1])
    taps_load = pltpu.make_async_copy(taps_hbm, taps_ref, const_sem.at[2])
    for load in (*edges, fine_load, coarse_load, taps_load, *bodies):
        load.start()

    barrier = pltpu.get_barrier_semaphore()

    def greet(w, carry):
        others = peers(w, feed, time)

        @pl.when(w > 0)
        def _():
            pl.semaphore_signal(barrier, inc=1, device_id=others[0], device_id_type=MESH)

        for other in others[1:]:
            pl.semaphore_signal(barrier, inc=1, device_id=other, device_id_type=MESH)
        return carry

    lax.fori_loop(0, 4, greet, 0)

    upper = lax.broadcasted_iota(jnp.int32, (8, HALF), 0) < 4

    def make_table(q):
        fine_re, fine_im = fine_ref[q, 0], fine_ref[q, 1]

        def rows(w, carry):
            owners = [f * TIMES + t for f, t in peers(w, feed, time)]
            for group in range(8):
                parts = []
                for side in range(2):
                    two = owners[group * 4 + side * 2:group * 4 + side * 2 + 2]
                    phase = [[coarse_ref[c, pl.ds(d, 1), :] for c in range(2)] for d in two]
                    a_re, a_im = [jnp.where(upper, phase[0][c], phase[1][c]) for c in range(2)]
                    parts.append((a_re * fine_re - a_im * fine_im, a_re * fine_im + a_im * fine_re))
                for c in range(2):
                    value = jnp.concatenate([parts[0][c], parts[1][c]], axis=0)
                    high = value.astype(jnp.bfloat16)
                    low = (value - high.astype(jnp.float32)).astype(jnp.bfloat16)
                    table[q, w, 0, c, group * 16:(group + 1) * 16, :] = high
                    table[q, w, 1, c, group * 16:(group + 1) * 16, :] = low
            return carry

        lax.fori_loop(0, 4, rows, 0)

    def halo_copy(o):
        return pltpu.make_async_remote_copy(
            src_ref=edge.at[o], dst_ref=halo.at[o], send_sem=halo_send.at[o], recv_sem=halo_recv.at[o],
            device_id=(feed, lax.rem(time + 1, TIMES)), device_id_type=MESH)

    def pack_edge(o):
        def block(nb, carry):
            lanes = pl.ds(pl.multiple_of(nb * LANES, LANES), LANES)
            for pair in range(8):
                two = []
                for side in range(2):
                    at = pl.multiple_of(tail + (pair * 2 + side) * FRAME + nb * LANES, LANES)
                    two.append(volt[o, :, pl.ds(at, LANES)].astype(jnp.float32))
                edge[o, pair, :, lanes] = jnp.concatenate(two, axis=0).astype(jnp.bfloat16)
            return carry

        lax.fori_loop(0, FRAME // LANES, block, 0)

    edges[0].wait()

    @pl.when(time < TIMES - 1)
    def _():
        pack_edge(0)

    pl.semaphore_wait(barrier, DEVICES - 1)
    edges[1].wait()

    @pl.when(time < TIMES - 1)
    def _():
        halo_copy(0).start()
        pack_edge(1)
        halo_copy(1).start()

    fine_load.wait()
    coarse_load.wait()
    make_table(0)

    @pl.when(time == 0)
    def _():
        halo[...] = jnp.zeros_like(halo)

    taps_load.wait()
    sublane = lax.broadcasted_iota(jnp.int32, (OCT, LANES), 0)

    def flags_of(o):
        flag = jnp.zeros((OCT, LANES), jnp.float32)
        for i in range(OCT):
            flag = jnp.where(sublane == i, flag_ref[o * OCT + i].astype(jnp.float32), flag)
        return flag

    def filter_blocks(o, nb, flag, blocks):
        for mb in blocks:
            sides = []
            for side in range(2):
                lane0 = nb * LANES + side * HALF
                lanes = pl.ds(pl.multiple_of(lane0, LANES), LANES)
                taps = [jnp.broadcast_to(taps_ref[pl.ds(p, 1), lanes], (OCT, LANES)) for p in range(TAPS)]
                sums = [None] * 16
                early = None
                for j in range(-15, 16):
                    if mb == 0 and j < 0:
                        pair, odd = (16 + j) // 2, (16 + j) % 2
                        if odd == 0 or early is None:
                            early = halo[o, pair, :, lanes].astype(jnp.float32)
                        x = early[odd * OCT:(odd + 1) * OCT]
                    else:
                        at = pl.multiple_of((mb * 16 + j) * FRAME + lane0, LANES)
                        x = volt[o, :, pl.ds(at, LANES)].astype(jnp.float32)
                    for m in range(max(0, j), min(15, j + 15) + 1):
                        term = taps[m - j] * x
                        sums[m] = term if sums[m] is None else sums[m] + term
                value = jnp.swapaxes(jnp.stack([s * flag for s in sums]), 0, 1)
                sides.append(value.astype(jnp.bfloat16).astype(jnp.float32))
            rows = slice(mb * 16, (mb + 1) * 16)
            lanes = pl.ds(pl.multiple_of(nb * LANES, LANES), LANES)
            folded[o, 0, :, rows, lanes] = (sides[0] + sides[1]).astype(jnp.bfloat16)
            folded[o, 1, :, rows, lanes] = (sides[0] - sides[1]).astype(jnp.bfloat16)

    lane = lax.broadcasted_iota(jnp.int32, (8, LANES), 1)
    left_half = lane < SPEC

    def exchange(o, q, step, other):
        return pltpu.make_async_remote_copy(
            src_ref=packed.at[step, o, q], dst_ref=out_ref.at[q, pl.ds(0, 2), time, feed, o],
            send_sem=send_sem, recv_sem=recv_sem, device_id=other, device_id_type=MESH)

    def own_copy(o, q):
        return pltpu.make_async_copy(packed.at[0, o, q], out_ref.at[q, pl.ds(0, 2), time, feed, o], own_sem)

    def octet(o, carry):
        flag = flags_of(o)

        def later_blocks(nb, c):
            filter_blocks(o, nb, flag, range(1, BLOCKS))
            return c

        def first_block(nb, c):
            filter_blocks(o, nb, flag, range(1))
            return c

        pltpu.make_async_copy(
            volt_hbm.at[pl.ds(0, OCT), pl.ds(0, tail)], volt.at[o, :, pl.ds(0, tail)], in_sem.at[o, 1]).wait()
        lax.fori_loop(0, 8, later_blocks, 0)

        @pl.when(time > 0)
        def _():
            halo_copy(o).wait_recv()

        lax.fori_loop(0, 8, first_block, 0)

        def parity(q, carry):
            @pl.when((o == 0) & (q == 1))
            def _():
                make_table(1)

            def section(w, carry):
                right = folded[o, q].reshape(OCT * SPEC, HALF)
                spectra[...] = lax.dot_general(
                    table[q, w].reshape(512, HALF), right, (((1,), (1,)), ((), ())),
                    preferred_element_type=jnp.float32).reshape(2, 2, 128, OCT * SPEC)

                def turn(g, c):
                    rows = pl.ds(pl.multiple_of(g * 8, 8), 8)
                    tiles = []
                    for pair in range(OCT // 2):
                        lanes = slice(pair * LANES, (pair + 1) * LANES)
                        re = spectra[0, 0, rows, lanes] + spectra[1, 0, rows, lanes]
                        im = spectra[0, 1, rows, lanes] + spectra[1, 1, rows, lanes]
                        tiles.append(jnp.where(left_half, re, pltpu.roll(im, SPEC, 1)))
                        tiles.append(jnp.where(left_half, pltpu.roll(re, SPEC, 1), im))
                    tile = jnp.swapaxes(jnp.stack(tiles), 0, 1)
                    packed[pl.ds(w * 32 + g * 2, 2), o, q] = tile.reshape(2, 2, 16, LANES).astype(jnp.bfloat16)
                    return c

                lax.fori_loop(0, 16, turn, 0, unroll=True)

                @pl.when(w == 0)
                def _():
                    own_copy(o, q).start()

                others = peers(w, feed, time)

                @pl.when(w > 0)
                def _():
                    exchange(o, q, w * 32, others[0]).start()

                for i in range(1, 32):
                    exchange(o, q, w * 32 + i, others[i]).start()
                return carry

            lax.fori_loop(0, 4, section, 0)
            return carry

        lax.fori_loop(0, 2, parity, 0)
        return carry

    lax.fori_loop(0, 2, octet, 0)

    @pl.when(time < TIMES - 1)
    def _():
        for o in range(2):
            halo_copy(o).wait_send()

    everything = pltpu.make_async_remote_copy(
        src_ref=packed.at[pl.ds(0, DEVICES - 1)], dst_ref=packed.at[pl.ds(0, DEVICES - 1)],
        send_sem=send_sem, recv_sem=recv_sem, device_id=(feed, time), device_id_type=MESH)
    everything.wait()
    own = packed.at[0]
    pltpu.make_async_copy(own, own, own_sem).wait()


def gather_spectra(voltages, pfb_taps, flags, coarse, fine):
    hbm = pl.BlockSpec(memory_space=pltpu.HBM)
    return pl.pallas_call(
        channelise,
        out_shape=jax.ShapeDtypeStruct((2, 2, TIMES, FEEDS, 2, 16, LANES), jnp.bfloat16),
        in_specs=[hbm, hbm, pl.BlockSpec(memory_space=pltpu.SMEM), hbm, hbm],
        out_specs=pl.BlockSpec(memory_space=pl.ANY),
        scratch_shapes=[
            pltpu.VMEM((2, OCT, SPEC * FRAME), jnp.int32),
            pltpu.VMEM((TAPS, FRAME), jnp.float32),
            pltpu.VMEM((2, DEVICES, HALF), jnp.float32),
            pltpu.VMEM((2, 2, 8, HALF), jnp.float32),
            pltpu.VMEM((2, 8, 16, FRAME), jnp.bfloat16),
            pltpu.VMEM((2, 8, 16, FRAME), jnp.bfloat16),
            pltpu.VMEM((2, 4, 2, 2, 128, HALF), jnp.bfloat16),
            pltpu.VMEM((2, 2, OCT, SPEC, HALF), jnp.bfloat16),
            pltpu.VMEM((2, 2, 128, OCT * SPEC), jnp.float32),
            pltpu.VMEM((DEVICES, 2, 2, 2, 16, LANES), jnp.bfloat16),
            pltpu.SemaphoreType.DMA((2, 2)),
            pltpu.SemaphoreType.DMA((3,)),
            pltpu.SemaphoreType.DMA((2,)),
            pltpu.SemaphoreType.DMA((2,)),
            pltpu.SemaphoreType.DMA,
            pltpu.SemaphoreType.DMA,
            pltpu.SemaphoreType.DMA,
        ],
        compiler_params=pltpu.CompilerParams(
            collective_id=0, has_side_effects=True, vmem_limit_bytes=48 << 20),
        name="channelise",
    )(voltages, pfb_taps, flags, coarse, fine)


def correlate(spec, out_hbm, left, right, result, out_sem):
    lane = lax.broadcasted_iota(jnp.int32, (1, LANES), 1)
    sign = jnp.where(lane < SPEC, 1.0, -1.0)
    dims = (((1,), (1,)), ((), ()))

    def put(step, j, c):
        q, p = step // 2, step % 2
        slot = step * 4 + j * 2 + c
        return pltpu.make_async_copy(result.at[slot], out_hbm.at[p, j, q, c], out_sem.at[slot])

    def channels(step, carry):
        q, p = step // 2, step % 2
        for j in range(2):
            for t in range(TIMES):
                tile = spec[q, p, t].astype(jnp.float32)
                tile = tile[:, :, j * OCT:(j + 1) * OCT, :].reshape(512, LANES)
                cols = slice(t * LANES, (t + 1) * LANES)
                right[j, :, cols] = tile.astype(jnp.bfloat16)
                left[j, :, cols] = (pltpu.roll(tile, SPEC, 1) * sign).astype(jnp.bfloat16)
            value = right[j]
            result[step * 4 + j * 2] = lax.dot_general(value, value, dims, preferred_element_type=jnp.float32)
            put(step, j, 0).start()
            result[step * 4 + j * 2 + 1] = lax.dot_general(left[j], value, dims, preferred_element_type=jnp.float32)
            put(step, j, 1).start()
        return carry

    lax.fori_loop(0, 4, channels, 0)
    for step in range(4):
        for j in range(2):
            for c in range(2):
                put(step, j, c).wait()


def visibilities(gathered):
    out = pl.pallas_call(
        correlate,
        out_shape=jax.ShapeDtypeStruct((2, 2, 2, 2, 512, 512), jnp.float32),
        in_specs=[pl.BlockSpec(memory_space=pltpu.VMEM)],
        out_specs=pl.BlockSpec(memory_space=pltpu.HBM),
        scratch_shapes=[
            pltpu.VMEM((2, 512, 512), jnp.bfloat16),
            pltpu.VMEM((2, 512, 512), jnp.bfloat16),
            pltpu.VMEM((16, 512, 512), jnp.float32),
            pltpu.SemaphoreType.DMA((16,)),
        ],
        compiler_params=pltpu.CompilerParams(vmem_limit_bytes=48 << 20),
        name="correlate",
    )(gathered)
    return out.reshape(8, 2, 512, 512)


def per_device(voltages, pfb_taps, feed_flags):
    coarse, fine = phase_tables()
    pinned = [
        pltpu.with_memory_space_constraint(x, pltpu.HBM)
        for x in (voltages, pfb_taps, feed_flags, jnp.asarray(coarse), jnp.asarray(fine))
    ]
    return visibilities(gather_spectra(*pinned))


def solution(mesh):
    return jax.shard_map(
        per_device,
        mesh=mesh,
        in_specs=(P("feed", "tm"), P(), P("feed")),
        out_specs=P(("feed", "tm"), None, None, None),
        check_vma=False,
    )
```

```python
import functools
import math

import jax
import jax.numpy as jnp
import numpy as np
from jax import lax
from jax.experimental import pallas as pl
from jax.experimental.pallas import tpu as pltpu
from jax.sharding import PartitionSpec as P

MESH = pl.DeviceIdType.MESH
LANES = 128
FRAME = 2048
HALF = FRAME // 2
TAPS = 16
FEEDS, TIMES = 32, 4
DEVICES = FEEDS * TIMES
SPEC = 64
OCT = 8
BLOCKS = SPEC // 16


def peers(section, feed, time):
    core, y, x, z = time % 2, feed // 16 * 2 + time // 2, feed // 4 % 4, feed % 4
    cores = [lax.rem(core + i, 2) for i in range(2)]
    ys = [lax.rem(y + i, 4) for i in range(4)]
    ys = [(lax.div(v, 2) * 16, lax.rem(v, 2) * 2) for v in ys]
    xs = [lax.rem(x + i, 4) * 4 for i in range(4)]
    zs = [lax.rem(z + i + 3 * section, 4) for i in range(4)]
    found = []
    for i in range(32):
        offset = i * 47 % DEVICES
        y_feed, y_time = ys[offset // 2 % 4]
        found.append((y_feed + xs[offset // 8 % 4] + zs[offset // 32], y_time + cores[offset % 2]))
    return found


def phase_tables():
    n = np.arange(HALF)
    coarse = np.exp(-2j * np.pi * ((8 * np.arange(DEVICES)[:, None] * n) % FRAME) / FRAME)
    rows = np.tile(2 * np.arange(4), 2)[None, :, None] + np.arange(2)[:, None, None]
    scale = 1.0 / (128 * 16 * math.sqrt(FRAME))
    fine = scale * np.exp(-2j * np.pi * (rows * n % FRAME) / FRAME)
    coarse = np.stack([coarse.real, coarse.imag]).astype(np.float32)
    fine = np.stack([fine.real, fine.imag], axis=1).astype(np.float32)
    return coarse, fine


def channelise(
    volt_hbm, taps_hbm, flag_ref, coarse_hbm, fine_hbm, out_ref,
    volt, taps_ref, coarse_ref, fine_ref, edge, halo, table, folded, spectra, packed,
    in_sem, const_sem, halo_send, halo_recv, send_sem, recv_sem, own_sem,
):
    feed, time = lax.axis_index("feed"), lax.axis_index("tm")

    tail = (SPEC - 16) * FRAME
    edges, bodies = [], []
    for o in range(2):
        inputs = pl.ds(o * OCT, OCT)
        edges.append(pltpu.make_async_copy(
            volt_hbm.at[inputs, pl.ds(tail, 16 * FRAME)], volt.at[o, :, pl.ds(tail, 16 * FRAME)], in_sem.at[o, 0]))
        bodies.append(pltpu.make_async_copy(
            volt_hbm.at[inputs, pl.ds(0, tail)], volt.at[o, :, pl.ds(0, tail)], in_sem.at[o, 1]))
    fine_load = pltpu.make_async_copy(fine_hbm, fine_ref, const_sem.at[0])
    coarse_load = pltpu.make_async_copy(coarse_hbm, coarse_ref, const_sem.at[1])
    taps_load = pltpu.make_async_copy(taps_hbm, taps_ref, const_sem.at[2])
    for load in (*edges, fine_load, coarse_load, taps_load, *bodies):
        load.start()

    barrier = pltpu.get_barrier_semaphore()

    def greet(w, carry):
        others = peers(w, feed, time)

        @pl.when(w > 0)
        def _():
            pl.semaphore_signal(barrier, inc=1, device_id=others[0], device_id_type=MESH)

        for other in others[1:]:
            pl.semaphore_signal(barrier, inc=1, device_id=other, device_id_type=MESH)
        return carry

    lax.fori_loop(0, 4, greet, 0)

    upper = lax.broadcasted_iota(jnp.int32, (8, HALF), 0) < 4

    def make_table(q):
        fine_re, fine_im = fine_ref[q, 0], fine_ref[q, 1]

        def rows(w, carry):
            owners = [f * TIMES + t for f, t in peers(w, feed, time)]
            for group in range(8):
                parts = []
                for side in range(2):
                    two = owners[group * 4 + side * 2:group * 4 + side * 2 + 2]
                    phase = [[coarse_ref[c, pl.ds(d, 1), :] for c in range(2)] for d in two]
                    a_re, a_im = [jnp.where(upper, phase[0][c], phase[1][c]) for c in range(2)]
                    parts.append((a_re * fine_re - a_im * fine_im, a_re * fine_im + a_im * fine_re))
                for c in range(2):
                    value = jnp.concatenate([parts[0][c], parts[1][c]], axis=0)
                    high = value.astype(jnp.bfloat16)
                    low = (value - high.astype(jnp.float32)).astype(jnp.bfloat16)
                    table[q, w, 0, c, group * 16:(group + 1) * 16, :] = high
                    table[q, w, 1, c, group * 16:(group + 1) * 16, :] = low
            return carry

        lax.fori_loop(0, 4, rows, 0)

    def halo_copy(o):
        return pltpu.make_async_remote_copy(
            src_ref=edge.at[o], dst_ref=halo.at[o], send_sem=halo_send.at[o], recv_sem=halo_recv.at[o],
            device_id=(feed, lax.rem(time + 1, TIMES)), device_id_type=MESH)

    across = lax.rem(feed + FEEDS // 2, FEEDS)
    relay = pltpu.make_async_remote_copy(
        src_ref=edge.at[1], dst_ref=edge.at[1], send_sem=halo_send.at[1], recv_sem=halo_recv.at[2],
        device_id=(across, 3), device_id_type=MESH)
    forward = pltpu.make_async_remote_copy(
        src_ref=edge.at[1], dst_ref=halo.at[1], send_sem=halo_send.at[1], recv_sem=halo_recv.at[1],
        device_id=(across, 2), device_id_type=MESH)

    def pack_edge(o):
        def block(nb, carry):
            lanes = pl.ds(pl.multiple_of(nb * LANES, LANES), LANES)
            for pair in range(8):
                two = []
                for side in range(2):
                    at = pl.multiple_of(tail + (pair * 2 + side) * FRAME + nb * LANES, LANES)
                    two.append(volt[o, :, pl.ds(at, LANES)].astype(jnp.float32))
                edge[o, pair, :, lanes] = jnp.concatenate(two, axis=0).astype(jnp.bfloat16)
            return carry

        lax.fori_loop(0, FRAME // LANES, block, 0)

    edges[0].wait()

    @pl.when(time < TIMES - 1)
    def _():
        pack_edge(0)

    pl.semaphore_wait(barrier, DEVICES - 1)
    edges[1].wait()

    @pl.when(time < TIMES - 1)
    def _():
        halo_copy(0).start()
        pack_edge(1)

    @pl.when((time == 0) | (time == 2))
    def _():
        halo_copy(1).start()

    @pl.when(time == 1)
    def _():
        relay.start()

    fine_load.wait()
    coarse_load.wait()
    make_table(0)

    @pl.when(time == 0)
    def _():
        halo[...] = jnp.zeros_like(halo)

    taps_load.wait()
    sublane = lax.broadcasted_iota(jnp.int32, (OCT, LANES), 0)

    def flags_of(o):
        flag = jnp.zeros((OCT, LANES), jnp.float32)
        for i in range(OCT):
            flag = jnp.where(sublane == i, flag_ref[o * OCT + i].astype(jnp.float32), flag)
        return flag

    def filter_blocks(o, nb, flag, blocks):
        for mb in blocks:
            sides = []
            for side in range(2):
                lane0 = nb * LANES + side * HALF
                lanes = pl.ds(pl.multiple_of(lane0, LANES), LANES)
                taps = [jnp.broadcast_to(taps_ref[pl.ds(p, 1), lanes], (OCT, LANES)) for p in range(TAPS)]
                sums = [None] * 16
                early = None
                for j in range(-15, 16):
                    if mb == 0 and j < 0:
                        pair, odd = (16 + j) // 2, (16 + j) % 2
                        if odd == 0 or early is None:
                            early = halo[o, pair, :, lanes].astype(jnp.float32)
                        x = early[odd * OCT:(odd + 1) * OCT]
                    else:
                        at = pl.multiple_of((mb * 16 + j) * FRAME + lane0, LANES)
                        x = volt[o, :, pl.ds(at, LANES)].astype(jnp.float32)
                    for m in range(max(0, j), min(15, j + 15) + 1):
                        term = taps[m - j] * x
                        sums[m] = term if sums[m] is None else sums[m] + term
                value = jnp.swapaxes(jnp.stack([s * flag for s in sums]), 0, 1)
                sides.append(value.astype(jnp.bfloat16).astype(jnp.float32))
            rows = slice(mb * 16, (mb + 1) * 16)
            lanes = pl.ds(pl.multiple_of(nb * LANES, LANES), LANES)
            folded[o, 0, :, rows, lanes] = (sides[0] + sides[1]).astype(jnp.bfloat16)
            folded[o, 1, :, rows, lanes] = (sides[0] - sides[1]).astype(jnp.bfloat16)

    lane = lax.broadcasted_iota(jnp.int32, (8, LANES), 1)
    left_half = lane < SPEC

    def exchange(o, q, step, other):
        return pltpu.make_async_remote_copy(
            src_ref=packed.at[step, o, q], dst_ref=out_ref.at[q, pl.ds(0, 2), time, feed, o],
            send_sem=send_sem, recv_sem=recv_sem, device_id=other, device_id_type=MESH)

    def own_copy(o, q):
        return pltpu.make_async_copy(packed.at[0, o, q], out_ref.at[q, pl.ds(0, 2), time, feed, o], own_sem)

    def octet(o, carry):
        flag = flags_of(o)

        def later_blocks(nb, c):
            filter_blocks(o, nb, flag, range(1, BLOCKS))
            return c

        def first_block(nb, c):
            filter_blocks(o, nb, flag, range(1))
            return c

        pltpu.make_async_copy(
            volt_hbm.at[pl.ds(0, OCT), pl.ds(0, tail)], volt.at[o, :, pl.ds(0, tail)], in_sem.at[o, 1]).wait()
        lax.fori_loop(0, 8, later_blocks, 0)

        @pl.when((time == 3) & (o == 0))
        def _():
            relay.wait_recv()
            forward.start()

        @pl.when(time > 0)
        def _():
            halo_copy(o).wait_recv()

        lax.fori_loop(0, 8, first_block, 0)

        def parity(q, carry):
            @pl.when((o == 0) & (q == 1))
            def _():
                make_table(1)

            def section(w, carry):
                right = folded[o, q].reshape(OCT * SPEC, HALF)
                spectra[...] = lax.dot_general(
                    table[q, w].reshape(512, HALF), right, (((1,), (1,)), ((), ())),
                    preferred_element_type=jnp.float32).reshape(2, 2, 128, OCT * SPEC)

                def turn(g, c):
                    rows = pl.ds(pl.multiple_of(g * 8, 8), 8)
                    tiles = []
                    for pair in range(OCT // 2):
                        lanes = slice(pair * LANES, (pair + 1) * LANES)
                        re = spectra[0, 0, rows, lanes] + spectra[1, 0, rows, lanes]
                        im = spectra[0, 1, rows, lanes] + spectra[1, 1, rows, lanes]
                        tiles.append(jnp.where(left_half, re, pltpu.roll(im, SPEC, 1)))
                        tiles.append(jnp.where(left_half, pltpu.roll(re, SPEC, 1), im))
                    tile = jnp.swapaxes(jnp.stack(tiles), 0, 1)
                    packed[pl.ds(w * 32 + g * 2, 2), o, q] = tile.reshape(2, 2, 16, LANES).astype(jnp.bfloat16)
                    return c

                lax.fori_loop(0, 16, turn, 0, unroll=True)

                @pl.when(w == 0)
                def _():
                    own_copy(o, q).start()

                others = peers(w, feed, time)

                @pl.when(w > 0)
                def _():
                    exchange(o, q, w * 32, others[0]).start()

                for i in range(1, 32):
                    exchange(o, q, w * 32 + i, others[i]).start()
                return carry

            lax.fori_loop(0, 4, section, 0)
            return carry

        lax.fori_loop(0, 2, parity, 0)
        return carry

    lax.fori_loop(0, 2, octet, 0)

    @pl.when(time < TIMES - 1)
    def _():
        halo_copy(0).wait_send()

    forward.wait_send()

    everything = pltpu.make_async_remote_copy(
        src_ref=packed.at[pl.ds(0, DEVICES - 1)], dst_ref=packed.at[pl.ds(0, DEVICES - 1)],
        send_sem=send_sem, recv_sem=recv_sem, device_id=(feed, time), device_id_type=MESH)
    everything.wait()
    own = packed.at[0]
    pltpu.make_async_copy(own, own, own_sem).wait()


def gather_spectra(voltages, pfb_taps, flags, coarse, fine):
    hbm = pl.BlockSpec(memory_space=pltpu.HBM)
    return pl.pallas_call(
        channelise,
        out_shape=jax.ShapeDtypeStruct((2, 2, TIMES, FEEDS, 2, 16, LANES), jnp.bfloat16),
        in_specs=[hbm, hbm, pl.BlockSpec(memory_space=pltpu.SMEM), hbm, hbm],
        out_specs=pl.BlockSpec(memory_space=pl.ANY),
        scratch_shapes=[
            pltpu.VMEM((2, OCT, SPEC * FRAME), jnp.int32),
            pltpu.VMEM((TAPS, FRAME), jnp.float32),
            pltpu.VMEM((2, DEVICES, HALF), jnp.float32),
            pltpu.VMEM((2, 2, 8, HALF), jnp.float32),
            pltpu.VMEM((2, 8, 16, FRAME), jnp.bfloat16),
            pltpu.VMEM((2, 8, 16, FRAME), jnp.bfloat16),
            pltpu.VMEM((2, 4, 2, 2, 128, HALF), jnp.bfloat16),
            pltpu.VMEM((2, 2, OCT, SPEC, HALF), jnp.bfloat16),
            pltpu.VMEM((2, 2, 128, OCT * SPEC), jnp.float32),
            pltpu.VMEM((DEVICES, 2, 2, 2, 16, LANES), jnp.bfloat16),
            pltpu.SemaphoreType.DMA((2, 2)),
            pltpu.SemaphoreType.DMA((3,)),
            pltpu.SemaphoreType.DMA((2,)),
            pltpu.SemaphoreType.DMA((3,)),
            pltpu.SemaphoreType.DMA,
            pltpu.SemaphoreType.DMA,
            pltpu.SemaphoreType.DMA,
        ],
        compiler_params=pltpu.CompilerParams(
            collective_id=0, has_side_effects=True, vmem_limit_bytes=48 << 20),
        name="channelise",
    )(voltages, pfb_taps, flags, coarse, fine)


def correlate(spec, out_hbm, left, right, result, out_sem):
    lane = lax.broadcasted_iota(jnp.int32, (1, LANES), 1)
    sign = jnp.where(lane < SPEC, 1.0, -1.0)
    dims = (((1,), (1,)), ((), ()))

    def put(step, j, c):
        q, p = step // 2, step % 2
        slot = step * 4 + j * 2 + c
        return pltpu.make_async_copy(result.at[slot], out_hbm.at[p, j, q, c], out_sem.at[slot])

    def channels(step, carry):
        q, p = step // 2, step % 2
        for j in range(2):
            for t in range(TIMES):
                tile = spec[q, p, t].astype(jnp.float32)
                tile = tile[:, :, j * OCT:(j + 1) * OCT, :].reshape(512, LANES)
                cols = slice(t * LANES, (t + 1) * LANES)
                right[j, :, cols] = tile.astype(jnp.bfloat16)
                left[j, :, cols] = (pltpu.roll(tile, SPEC, 1) * sign).astype(jnp.bfloat16)
            value = right[j]
            result[step * 4 + j * 2] = lax.dot_general(value, value, dims, preferred_element_type=jnp.float32)
            put(step, j, 0).start()
            result[step * 4 + j * 2 + 1] = lax.dot_general(left[j], value, dims, preferred_element_type=jnp.float32)
            put(step, j, 1).start()
        return carry

    lax.fori_loop(0, 4, channels, 0)
    for step in range(4):
        for j in range(2):
            for c in range(2):
                put(step, j, c).wait()


def visibilities(gathered):
    out = pl.pallas_call(
        correlate,
        out_shape=jax.ShapeDtypeStruct((2, 2, 2, 2, 512, 512), jnp.float32),
        in_specs=[pl.BlockSpec(memory_space=pltpu.VMEM)],
        out_specs=pl.BlockSpec(memory_space=pltpu.HBM),
        scratch_shapes=[
            pltpu.VMEM((2, 512, 512), jnp.bfloat16),
            pltpu.VMEM((2, 512, 512), jnp.bfloat16),
            pltpu.VMEM((16, 512, 512), jnp.float32),
            pltpu.SemaphoreType.DMA((16,)),
        ],
        compiler_params=pltpu.CompilerParams(vmem_limit_bytes=48 << 20),
        name="correlate",
    )(gathered)
    return out.reshape(8, 2, 512, 512)


def per_device(voltages, pfb_taps, feed_flags):
    coarse, fine = phase_tables()
    pinned = [
        pltpu.with_memory_space_constraint(x, pltpu.HBM)
        for x in (voltages, pfb_taps, feed_flags, jnp.asarray(coarse), jnp.asarray(fine))
    ]
    return visibilities(gather_spectra(*pinned))


def solution(mesh):
    return jax.shard_map(
        per_device,
        mesh=mesh,
        in_specs=(P("feed", "tm"), P(), P("feed")),
        out_specs=P(("feed", "tm"), None, None, None),
        check_vma=False,
    )
```

```python
import functools
import math

import jax
import jax.numpy as jnp
import numpy as np
from jax import lax
from jax.experimental import pallas as pl
from jax.experimental.pallas import tpu as pltpu
from jax.sharding import PartitionSpec as P

MESH = pl.DeviceIdType.MESH
LANES = 128
FRAME = 2048
HALF = FRAME // 2
TAPS = 16
FEEDS, TIMES = 32, 4
DEVICES = FEEDS * TIMES
SPEC = 64
OCT = 8
BLOCKS = SPEC // 16
DETOUR = 5


def peers(section, feed, time):
    core, y, x, z = time % 2, feed // 16 * 2 + time // 2, feed // 4 % 4, feed % 4
    cores = [lax.rem(core + i, 2) for i in range(2)]
    ys = [lax.rem(y + i, 4) for i in range(4)]
    ys = [(lax.div(v, 2) * 16, lax.rem(v, 2) * 2) for v in ys]
    xs = [lax.rem(x + i, 4) * 4 for i in range(4)]
    zs = [lax.rem(z + i + 3 * section, 4) for i in range(4)]
    found = []
    for i in range(32):
        offset = i * 47 % DEVICES
        y_feed, y_time = ys[offset // 2 % 4]
        found.append((y_feed + xs[offset // 8 % 4] + zs[offset // 32], y_time + cores[offset % 2]))
    return found


def phase_tables():
    n = np.arange(HALF)
    coarse = np.exp(-2j * np.pi * ((8 * np.arange(DEVICES)[:, None] * n) % FRAME) / FRAME)
    rows = np.tile(2 * np.arange(4), 2)[None, :, None] + np.arange(2)[:, None, None]
    scale = 1.0 / (128 * 16 * math.sqrt(FRAME))
    fine = scale * np.exp(-2j * np.pi * (rows * n % FRAME) / FRAME)
    coarse = np.stack([coarse.real, coarse.imag]).astype(np.float32)
    fine = np.stack([fine.real, fine.imag], axis=1).astype(np.float32)
    return coarse, fine


def channelise(
    volt_hbm, taps_hbm, flag_ref, coarse_hbm, fine_hbm, out_ref,
    volt, taps_ref, coarse_ref, fine_ref, edge, halo, table, folded, spectra, packed,
    in_sem, const_sem, halo_send, halo_recv, send_sem, recv_sem, own_sem,
):
    feed, time = lax.axis_index("feed"), lax.axis_index("tm")

    tail = (SPEC - 16) * FRAME
    edges, bodies = [], []
    for o in range(2):
        inputs = pl.ds(o * OCT, OCT)
        edges.append(pltpu.make_async_copy(
            volt_hbm.at[inputs, pl.ds(tail, 16 * FRAME)], volt.at[o, :, pl.ds(tail, 16 * FRAME)], in_sem.at[o, 0]))
        bodies.append(pltpu.make_async_copy(
            volt_hbm.at[inputs, pl.ds(0, tail)], volt.at[o, :, pl.ds(0, tail)], in_sem.at[o, 1]))
    fine_load = pltpu.make_async_copy(fine_hbm, fine_ref, const_sem.at[0])
    coarse_load = pltpu.make_async_copy(coarse_hbm, coarse_ref, const_sem.at[1])
    taps_load = pltpu.make_async_copy(taps_hbm, taps_ref, const_sem.at[2])
    for load in (*edges, fine_load, coarse_load, taps_load, *bodies):
        load.start()

    barrier = pltpu.get_barrier_semaphore()

    def greet(w, carry):
        others = peers(w, feed, time)

        @pl.when(w > 0)
        def _():
            pl.semaphore_signal(barrier, inc=1, device_id=others[0], device_id_type=MESH)

        for other in others[1:]:
            pl.semaphore_signal(barrier, inc=1, device_id=other, device_id_type=MESH)
        return carry

    lax.fori_loop(0, 4, greet, 0)

    upper = lax.broadcasted_iota(jnp.int32, (8, HALF), 0) < 4

    def make_table(q):
        fine_re, fine_im = fine_ref[q, 0], fine_ref[q, 1]

        def rows(w, carry):
            owners = [f * TIMES + t for f, t in peers(w, feed, time)]
            for group in range(8):
                parts = []
                for side in range(2):
                    two = owners[group * 4 + side * 2:group * 4 + side * 2 + 2]
                    phase = [[coarse_ref[c, pl.ds(d, 1), :] for c in range(2)] for d in two]
                    a_re, a_im = [jnp.where(upper, phase[0][c], phase[1][c]) for c in range(2)]
                    parts.append((a_re * fine_re - a_im * fine_im, a_re * fine_im + a_im * fine_re))
                for c in range(2):
                    value = jnp.concatenate([parts[0][c], parts[1][c]], axis=0)
                    high = value.astype(jnp.bfloat16)
                    low = (value - high.astype(jnp.float32)).astype(jnp.bfloat16)
                    table[q, w, 0, c, group * 16:(group + 1) * 16, :] = high
                    table[q, w, 1, c, group * 16:(group + 1) * 16, :] = low
            return carry

        lax.fori_loop(0, 4, rows, 0)

    def halo_copy(o):
        return pltpu.make_async_remote_copy(
            src_ref=edge.at[o], dst_ref=halo.at[o], send_sem=halo_send.at[o], recv_sem=halo_recv.at[o],
            device_id=(feed, lax.rem(time + 1, TIMES)), device_id_type=MESH)

    across = lax.rem(feed + FEEDS // 2, FEEDS)
    detour, straight = pl.ds(0, DETOUR), pl.ds(DETOUR, 8 - DETOUR)
    relay = pltpu.make_async_remote_copy(
        src_ref=edge.at[1, detour], dst_ref=edge.at[1, detour],
        send_sem=halo_send.at[2], recv_sem=halo_recv.at[2], device_id=(across, 3), device_id_type=MESH)
    forward = pltpu.make_async_remote_copy(
        src_ref=edge.at[1, detour], dst_ref=halo.at[1, detour],
        send_sem=halo_send.at[2], recv_sem=halo_recv.at[1], device_id=(across, 2), device_id_type=MESH)
    rest = pltpu.make_async_remote_copy(
        src_ref=edge.at[1, straight], dst_ref=halo.at[1, straight],
        send_sem=halo_send.at[1], recv_sem=halo_recv.at[1], device_id=(feed, 2), device_id_type=MESH)

    def pack_edge(o):
        def block(nb, carry):
            lanes = pl.ds(pl.multiple_of(nb * LANES, LANES), LANES)
            for pair in range(8):
                two = []
                for side in range(2):
                    at = pl.multiple_of(tail + (pair * 2 + side) * FRAME + nb * LANES, LANES)
                    two.append(volt[o, :, pl.ds(at, LANES)].astype(jnp.float32))
                edge[o, pair, :, lanes] = jnp.concatenate(two, axis=0).astype(jnp.bfloat16)
            return carry

        lax.fori_loop(0, FRAME // LANES, block, 0)

    edges[0].wait()

    @pl.when(time < TIMES - 1)
    def _():
        pack_edge(0)

    pl.semaphore_wait(barrier, DEVICES - 1)
    edges[1].wait()

    @pl.when(time < TIMES - 1)
    def _():
        halo_copy(0).start()
        pack_edge(1)

    @pl.when((time == 0) | (time == 2))
    def _():
        halo_copy(1).start()

    @pl.when(time == 1)
    def _():
        relay.start()
        rest.start()

    fine_load.wait()
    coarse_load.wait()
    make_table(0)

    @pl.when(time == 0)
    def _():
        halo[...] = jnp.zeros_like(halo)

    taps_load.wait()
    sublane = lax.broadcasted_iota(jnp.int32, (OCT, LANES), 0)

    def flags_of(o):
        flag = jnp.zeros((OCT, LANES), jnp.float32)
        for i in range(OCT):
            flag = jnp.where(sublane == i, flag_ref[o * OCT + i].astype(jnp.float32), flag)
        return flag

    def filter_blocks(o, nb, flag, blocks):
        for mb in blocks:
            sides = []
            for side in range(2):
                lane0 = nb * LANES + side * HALF
                lanes = pl.ds(pl.multiple_of(lane0, LANES), LANES)
                taps = [jnp.broadcast_to(taps_ref[pl.ds(p, 1), lanes], (OCT, LANES)) for p in range(TAPS)]
                sums = [None] * 16
                early = None
                for j in range(-15, 16):
                    if mb == 0 and j < 0:
                        pair, odd = (16 + j) // 2, (16 + j) % 2
                        if odd == 0 or early is None:
                            early = halo[o, pair, :, lanes].astype(jnp.float32)
                        x = early[odd * OCT:(odd + 1) * OCT]
                    else:
                        at = pl.multiple_of((mb * 16 + j) * FRAME + lane0, LANES)
                        x = volt[o, :, pl.ds(at, LANES)].astype(jnp.float32)
                    for m in range(max(0, j), min(15, j + 15) + 1):
                        term = taps[m - j] * x
                        sums[m] = term if sums[m] is None else sums[m] + term
                value = jnp.swapaxes(jnp.stack([s * flag for s in sums]), 0, 1)
                sides.append(value.astype(jnp.bfloat16).astype(jnp.float32))
            rows = slice(mb * 16, (mb + 1) * 16)
            lanes = pl.ds(pl.multiple_of(nb * LANES, LANES), LANES)
            folded[o, 0, :, rows, lanes] = (sides[0] + sides[1]).astype(jnp.bfloat16)
            folded[o, 1, :, rows, lanes] = (sides[0] - sides[1]).astype(jnp.bfloat16)

    lane = lax.broadcasted_iota(jnp.int32, (8, LANES), 1)
    left_half = lane < SPEC

    def exchange(o, q, step, other):
        return pltpu.make_async_remote_copy(
            src_ref=packed.at[step, o, q], dst_ref=out_ref.at[q, pl.ds(0, 2), time, feed, o],
            send_sem=send_sem, recv_sem=recv_sem, device_id=other, device_id_type=MESH)

    def own_copy(o, q):
        return pltpu.make_async_copy(packed.at[0, o, q], out_ref.at[q, pl.ds(0, 2), time, feed, o], own_sem)

    def octet(o, carry):
        flag = flags_of(o)

        def later_blocks(nb, c):
            filter_blocks(o, nb, flag, range(1, BLOCKS))
            return c

        def first_block(nb, c):
            filter_blocks(o, nb, flag, range(1))
            return c

        pltpu.make_async_copy(
            volt_hbm.at[pl.ds(0, OCT), pl.ds(0, tail)], volt.at[o, :, pl.ds(0, tail)], in_sem.at[o, 1]).wait()
        lax.fori_loop(0, 8, later_blocks, 0)

        @pl.when((time == 3) & (o == 0))
        def _():
            relay.wait_recv()
            forward.start()

        @pl.when(time > 0)
        def _():
            halo_copy(o).wait_recv()

        lax.fori_loop(0, 8, first_block, 0)

        def parity(q, carry):
            @pl.when((o == 0) & (q == 1))
            def _():
                make_table(1)

            def section(w, carry):
                right = folded[o, q].reshape(OCT * SPEC, HALF)
                spectra[...] = lax.dot_general(
                    table[q, w].reshape(512, HALF), right, (((1,), (1,)), ((), ())),
                    preferred_element_type=jnp.float32).reshape(2, 2, 128, OCT * SPEC)

                def turn(g, c):
                    rows = pl.ds(pl.multiple_of(g * 8, 8), 8)
                    tiles = []
                    for pair in range(OCT // 2):
                        lanes = slice(pair * LANES, (pair + 1) * LANES)
                        re = spectra[0, 0, rows, lanes] + spectra[1, 0, rows, lanes]
                        im = spectra[0, 1, rows, lanes] + spectra[1, 1, rows, lanes]
                        tiles.append(jnp.where(left_half, re, pltpu.roll(im, SPEC, 1)))
                        tiles.append(jnp.where(left_half, pltpu.roll(re, SPEC, 1), im))
                    tile = jnp.swapaxes(jnp.stack(tiles), 0, 1)
                    packed[pl.ds(w * 32 + g * 2, 2), o, q] = tile.reshape(2, 2, 16, LANES).astype(jnp.bfloat16)
                    return c

                lax.fori_loop(0, 16, turn, 0, unroll=True)

                @pl.when(w == 0)
                def _():
                    own_copy(o, q).start()

                others = peers(w, feed, time)

                @pl.when(w > 0)
                def _():
                    exchange(o, q, w * 32, others[0]).start()

                for i in range(1, 32):
                    exchange(o, q, w * 32 + i, others[i]).start()
                return carry

            lax.fori_loop(0, 4, section, 0)
            return carry

        lax.fori_loop(0, 2, parity, 0)
        return carry

    lax.fori_loop(0, 2, octet, 0)

    @pl.when(time < TIMES - 1)
    def _():
        halo_copy(0).wait_send()

    @pl.when((time == 0) | (time == 2))
    def _():
        halo_copy(1).wait_send()

    @pl.when(time == 1)
    def _():
        relay.wait_send()
        rest.wait_send()

    @pl.when(time == 3)
    def _():
        forward.wait_send()

    everything = pltpu.make_async_remote_copy(
        src_ref=packed.at[pl.ds(0, DEVICES - 1)], dst_ref=packed.at[pl.ds(0, DEVICES - 1)],
        send_sem=send_sem, recv_sem=recv_sem, device_id=(feed, time), device_id_type=MESH)
    everything.wait()
    own = packed.at[0]
    pltpu.make_async_copy(own, own, own_sem).wait()


def gather_spectra(voltages, pfb_taps, flags, coarse, fine):
    hbm = pl.BlockSpec(memory_space=pltpu.HBM)
    return pl.pallas_call(
        channelise,
        out_shape=jax.ShapeDtypeStruct((2, 2, TIMES, FEEDS, 2, 16, LANES), jnp.bfloat16),
        in_specs=[hbm, hbm, pl.BlockSpec(memory_space=pltpu.SMEM), hbm, hbm],
        out_specs=pl.BlockSpec(memory_space=pl.ANY),
        scratch_shapes=[
            pltpu.VMEM((2, OCT, SPEC * FRAME), jnp.int32),
            pltpu.VMEM((TAPS, FRAME), jnp.float32),
            pltpu.VMEM((2, DEVICES, HALF), jnp.float32),
            pltpu.VMEM((2, 2, 8, HALF), jnp.float32),
            pltpu.VMEM((2, 8, 16, FRAME), jnp.bfloat16),
            pltpu.VMEM((2, 8, 16, FRAME), jnp.bfloat16),
            pltpu.VMEM((2, 4, 2, 2, 128, HALF), jnp.bfloat16),
            pltpu.VMEM((2, 2, OCT, SPEC, HALF), jnp.bfloat16),
            pltpu.VMEM((2, 2, 128, OCT * SPEC), jnp.float32),
            pltpu.VMEM((DEVICES, 2, 2, 2, 16, LANES), jnp.bfloat16),
            pltpu.SemaphoreType.DMA((2, 2)),
            pltpu.SemaphoreType.DMA((3,)),
            pltpu.SemaphoreType.DMA((3,)),
            pltpu.SemaphoreType.DMA((3,)),
            pltpu.SemaphoreType.DMA,
            pltpu.SemaphoreType.DMA,
            pltpu.SemaphoreType.DMA,
        ],
        compiler_params=pltpu.CompilerParams(
            collective_id=0, has_side_effects=True, vmem_limit_bytes=48 << 20),
        name="channelise",
    )(voltages, pfb_taps, flags, coarse, fine)


def correlate(spec, out_hbm, left, right, result, out_sem):
    lane = lax.broadcasted_iota(jnp.int32, (1, LANES), 1)
    sign = jnp.where(lane < SPEC, 1.0, -1.0)
    dims = (((1,), (1,)), ((), ()))

    def put(step, j, c):
        q, p = step // 2, step % 2
        slot = step * 4 + j * 2 + c
        return pltpu.make_async_copy(result.at[slot], out_hbm.at[p, j, q, c], out_sem.at[slot])

    def channels(step, carry):
        q, p = step // 2, step % 2
        for j in range(2):
            for t in range(TIMES):
                tile = spec[q, p, t].astype(jnp.float32)
                tile = tile[:, :, j * OCT:(j + 1) * OCT, :].reshape(512, LANES)
                cols = slice(t * LANES, (t + 1) * LANES)
                right[j, :, cols] = tile.astype(jnp.bfloat16)
                left[j, :, cols] = (pltpu.roll(tile, SPEC, 1) * sign).astype(jnp.bfloat16)
            value = right[j]
            result[step * 4 + j * 2] = lax.dot_general(value, value, dims, preferred_element_type=jnp.float32)
            put(step, j, 0).start()
            result[step * 4 + j * 2 + 1] = lax.dot_general(left[j], value, dims, preferred_element_type=jnp.float32)
            put(step, j, 1).start()
        return carry

    lax.fori_loop(0, 4, channels, 0)
    for step in range(4):
        for j in range(2):
            for c in range(2):
                put(step, j, c).wait()


def visibilities(gathered):
    out = pl.pallas_call(
        correlate,
        out_shape=jax.ShapeDtypeStruct((2, 2, 2, 2, 512, 512), jnp.float32),
        in_specs=[pl.BlockSpec(memory_space=pltpu.VMEM)],
        out_specs=pl.BlockSpec(memory_space=pltpu.HBM),
        scratch_shapes=[
            pltpu.VMEM((2, 512, 512), jnp.bfloat16),
            pltpu.VMEM((2, 512, 512), jnp.bfloat16),
            pltpu.VMEM((16, 512, 512), jnp.float32),
            pltpu.SemaphoreType.DMA((16,)),
        ],
        compiler_params=pltpu.CompilerParams(vmem_limit_bytes=48 << 20),
        name="correlate",
    )(gathered)
    return out.reshape(8, 2, 512, 512)


def per_device(voltages, pfb_taps, feed_flags):
    coarse, fine = phase_tables()
    pinned = [
        pltpu.with_memory_space_constraint(x, pltpu.HBM)
        for x in (voltages, pfb_taps, feed_flags, jnp.asarray(coarse), jnp.asarray(fine))
    ]
    return visibilities(gather_spectra(*pinned))


def solution(mesh):
    return jax.shard_map(
        per_device,
        mesh=mesh,
        in_specs=(P("feed", "tm"), P(), P("feed")),
        out_specs=P(("feed", "tm"), None, None, None),
        check_vma=False,
    )
```

```python
import functools
import math

import jax
import jax.numpy as jnp
import numpy as np
from jax import lax
from jax.experimental import pallas as pl
from jax.experimental.pallas import tpu as pltpu
from jax.sharding import PartitionSpec as P

MESH = pl.DeviceIdType.MESH
LANES = 128
FRAME = 2048
HALF = FRAME // 2
TAPS = 16
FEEDS, TIMES = 32, 4
DEVICES = FEEDS * TIMES
SPEC = 64
OCT = 8
BLOCKS = SPEC // 16
DETOUR = 5


def peers(section, feed, time):
    core, y, x, z = time % 2, feed // 16 * 2 + time // 2, feed // 4 % 4, feed % 4
    cores = [lax.rem(core + i, 2) for i in range(2)]
    ys = [lax.rem(y + i, 4) for i in range(4)]
    ys = [(lax.div(v, 2) * 16, lax.rem(v, 2) * 2) for v in ys]
    xs = [lax.rem(x + i, 4) * 4 for i in range(4)]
    zs = [lax.rem(z + i + 3 * section, 4) for i in range(4)]
    found = []
    for i in range(32):
        offset = i * 47 % DEVICES
        y_feed, y_time = ys[offset // 2 % 4]
        found.append((y_feed + xs[offset // 8 % 4] + zs[offset // 32], y_time + cores[offset % 2]))
    return found


def phase_tables():
    n = np.arange(HALF)
    coarse = np.exp(-2j * np.pi * ((8 * np.arange(DEVICES)[:, None] * n) % FRAME) / FRAME)
    rows = np.tile(2 * np.arange(4), 2)[None, :, None] + np.arange(2)[:, None, None]
    scale = 1.0 / (128 * 16 * math.sqrt(FRAME))
    fine = scale * np.exp(-2j * np.pi * (rows * n % FRAME) / FRAME)
    coarse = np.stack([coarse.real, coarse.imag]).astype(np.float32)
    fine = np.stack([fine.real, fine.imag], axis=1).astype(np.float32)
    return coarse, fine


def fir(taps, x, first, last):
    sums = {}
    for m in range(first, last + 1):
        total = taps[0] * x[m]
        for p in range(1, len(taps)):
            total = total + taps[p] * x[m - p]
        sums[m] = total
    return sums


def fast_fir(taps, x):
    h0, h1 = taps[0::2], taps[1::2]
    x0 = {j // 2: v for j, v in x.items() if j % 2 == 0}
    x1 = {j // 2: v for j, v in x.items() if j % 2 == 1}
    both = {r: x0[r] + x1[r] for r in range(-7, 8)}
    even = fir(h0, x0, 0, 7)
    odd = fir(h1, x1, -1, 7)
    mixed = fir([a + b for a, b in zip(h0, h1)], both, 0, 7)
    sums = []
    for r in range(8):
        sums.append(even[r] + odd[r - 1])
        sums.append(mixed[r] - (even[r] + odd[r]))
    return sums


def channelise(
    volt_hbm, taps_hbm, flag_ref, coarse_hbm, fine_hbm, out_ref,
    volt, taps_ref, coarse_ref, fine_ref, edge, halo, table, folded, spectra, packed,
    in_sem, const_sem, halo_send, halo_recv, send_sem, recv_sem, own_sem,
):
    feed, time = lax.axis_index("feed"), lax.axis_index("tm")

    tail = (SPEC - 16) * FRAME
    edges, bodies = [], []
    for o in range(2):
        inputs = pl.ds(o * OCT, OCT)
        edges.append(pltpu.make_async_copy(
            volt_hbm.at[inputs, pl.ds(tail, 16 * FRAME)], volt.at[o, :, pl.ds(tail, 16 * FRAME)], in_sem.at[o, 0]))
        bodies.append(pltpu.make_async_copy(
            volt_hbm.at[inputs, pl.ds(0, tail)], volt.at[o, :, pl.ds(0, tail)], in_sem.at[o, 1]))
    fine_load = pltpu.make_async_copy(fine_hbm, fine_ref, const_sem.at[0])
    coarse_load = pltpu.make_async_copy(coarse_hbm, coarse_ref, const_sem.at[1])
    taps_load = pltpu.make_async_copy(taps_hbm, taps_ref, const_sem.at[2])
    for load in (*edges, fine_load, coarse_load, taps_load, *bodies):
        load.start()

    barrier = pltpu.get_barrier_semaphore()

    def greet(w, carry):
        others = peers(w, feed, time)

        @pl.when(w > 0)
        def _():
            pl.semaphore_signal(barrier, inc=1, device_id=others[0], device_id_type=MESH)

        for other in others[1:]:
            pl.semaphore_signal(barrier, inc=1, device_id=other, device_id_type=MESH)
        return carry

    lax.fori_loop(0, 4, greet, 0)

    upper = lax.broadcasted_iota(jnp.int32, (8, HALF), 0) < 4

    def make_table(q):
        fine_re, fine_im = fine_ref[q, 0], fine_ref[q, 1]

        def rows(w, carry):
            owners = [f * TIMES + t for f, t in peers(w, feed, time)]
            for group in range(8):
                parts = []
                for side in range(2):
                    two = owners[group * 4 + side * 2:group * 4 + side * 2 + 2]
                    phase = [[coarse_ref[c, pl.ds(d, 1), :] for c in range(2)] for d in two]
                    a_re, a_im = [jnp.where(upper, phase[0][c], phase[1][c]) for c in range(2)]
                    parts.append((a_re * fine_re - a_im * fine_im, a_re * fine_im + a_im * fine_re))
                for c in range(2):
                    value = jnp.concatenate([parts[0][c], parts[1][c]], axis=0)
                    high = value.astype(jnp.bfloat16)
                    low = (value - high.astype(jnp.float32)).astype(jnp.bfloat16)
                    table[q, w, 0, c, group * 16:(group + 1) * 16, :] = high
                    table[q, w, 1, c, group * 16:(group + 1) * 16, :] = low
            return carry

        lax.fori_loop(0, 4, rows, 0)

    def halo_copy(o):
        return pltpu.make_async_remote_copy(
            src_ref=edge.at[o], dst_ref=halo.at[o], send_sem=halo_send.at[o], recv_sem=halo_recv.at[o],
            device_id=(feed, lax.rem(time + 1, TIMES)), device_id_type=MESH)

    across = lax.rem(feed + FEEDS // 2, FEEDS)
    detour, straight = pl.ds(0, DETOUR), pl.ds(DETOUR, 8 - DETOUR)
    relay = pltpu.make_async_remote_copy(
        src_ref=edge.at[1, detour], dst_ref=edge.at[1, detour],
        send_sem=halo_send.at[2], recv_sem=halo_recv.at[2], device_id=(across, 3), device_id_type=MESH)
    forward = pltpu.make_async_remote_copy(
        src_ref=edge.at[1, detour], dst_ref=halo.at[1, detour],
        send_sem=halo_send.at[2], recv_sem=halo_recv.at[1], device_id=(across, 2), device_id_type=MESH)
    rest = pltpu.make_async_remote_copy(
        src_ref=edge.at[1, straight], dst_ref=halo.at[1, straight],
        send_sem=halo_send.at[1], recv_sem=halo_recv.at[1], device_id=(feed, 2), device_id_type=MESH)

    def pack_edge(o):
        def block(nb, carry):
            lanes = pl.ds(pl.multiple_of(nb * LANES, LANES), LANES)
            for pair in range(8):
                two = []
                for side in range(2):
                    at = pl.multiple_of(tail + (pair * 2 + side) * FRAME + nb * LANES, LANES)
                    two.append(volt[o, :, pl.ds(at, LANES)].astype(jnp.float32))
                edge[o, pair, :, lanes] = jnp.concatenate(two, axis=0).astype(jnp.bfloat16)
            return carry

        lax.fori_loop(0, FRAME // LANES, block, 0)

    edges[0].wait()

    @pl.when(time < TIMES - 1)
    def _():
        pack_edge(0)

    pl.semaphore_wait(barrier, DEVICES - 1)
    edges[1].wait()

    @pl.when(time < TIMES - 1)
    def _():
        halo_copy(0).start()
        pack_edge(1)

    @pl.when((time == 0) | (time == 2))
    def _():
        halo_copy(1).start()

    @pl.when(time == 1)
    def _():
        relay.start()
        rest.start()

    fine_load.wait()
    coarse_load.wait()
    make_table(0)

    @pl.when(time == 0)
    def _():
        halo[...] = jnp.zeros_like(halo)

    taps_load.wait()
    sublane = lax.broadcasted_iota(jnp.int32, (OCT, LANES), 0)

    def flags_of(o):
        flag = jnp.zeros((OCT, LANES), jnp.float32)
        for i in range(OCT):
            flag = jnp.where(sublane == i, flag_ref[o * OCT + i].astype(jnp.float32), flag)
        return flag

    def filter_blocks(o, nb, flag, blocks):
        for mb in blocks:
            sides = []
            for side in range(2):
                lane0 = nb * LANES + side * HALF
                lanes = pl.ds(pl.multiple_of(lane0, LANES), LANES)
                taps = [jnp.broadcast_to(taps_ref[pl.ds(p, 1), lanes], (OCT, LANES)) for p in range(TAPS)]
                x = {}
                for j in range(-15, 16):
                    if mb == 0 and j < 0:
                        pair, odd = (16 + j) // 2, (16 + j) % 2
                        x[j] = halo[o, pair, :, lanes].astype(jnp.float32)[odd * OCT:(odd + 1) * OCT]
                    else:
                        at = pl.multiple_of((mb * 16 + j) * FRAME + lane0, LANES)
                        x[j] = volt[o, :, pl.ds(at, LANES)].astype(jnp.float32)
                sums = fast_fir(taps, x)
                value = jnp.swapaxes(jnp.stack([s * flag for s in sums]), 0, 1)
                sides.append(value.astype(jnp.bfloat16).astype(jnp.float32))
            rows = slice(mb * 16, (mb + 1) * 16)
            lanes = pl.ds(pl.multiple_of(nb * LANES, LANES), LANES)
            folded[o, 0, :, rows, lanes] = (sides[0] + sides[1]).astype(jnp.bfloat16)
            folded[o, 1, :, rows, lanes] = (sides[0] - sides[1]).astype(jnp.bfloat16)

    lane = lax.broadcasted_iota(jnp.int32, (8, LANES), 1)
    left_half = lane < SPEC

    def exchange(o, q, step, other):
        return pltpu.make_async_remote_copy(
            src_ref=packed.at[step, o, q], dst_ref=out_ref.at[q, pl.ds(0, 2), time, feed, o],
            send_sem=send_sem, recv_sem=recv_sem, device_id=other, device_id_type=MESH)

    def own_copy(o, q):
        return pltpu.make_async_copy(packed.at[0, o, q], out_ref.at[q, pl.ds(0, 2), time, feed, o], own_sem)

    def octet(o, carry):
        flag = flags_of(o)

        def later_blocks(nb, c):
            filter_blocks(o, nb, flag, range(1, BLOCKS))
            return c

        def first_block(nb, c):
            filter_blocks(o, nb, flag, range(1))
            return c

        pltpu.make_async_copy(
            volt_hbm.at[pl.ds(0, OCT), pl.ds(0, tail)], volt.at[o, :, pl.ds(0, tail)], in_sem.at[o, 1]).wait()
        lax.fori_loop(0, 8, later_blocks, 0)

        @pl.when((time == 3) & (o == 0))
        def _():
            relay.wait_recv()
            forward.start()

        @pl.when(time > 0)
        def _():
            halo_copy(o).wait_recv()

        lax.fori_loop(0, 8, first_block, 0)

        def parity(q, carry):
            @pl.when((o == 0) & (q == 1))
            def _():
                make_table(1)

            def section(w, carry):
                right = folded[o, q].reshape(OCT * SPEC, HALF)
                spectra[...] = lax.dot_general(
                    table[q, w].reshape(512, HALF), right, (((1,), (1,)), ((), ())),
                    preferred_element_type=jnp.float32).reshape(2, 2, 128, OCT * SPEC)

                def turn(g, c):
                    rows = pl.ds(pl.multiple_of(g * 8, 8), 8)
                    tiles = []
                    for pair in range(OCT // 2):
                        lanes = slice(pair * LANES, (pair + 1) * LANES)
                        re = spectra[0, 0, rows, lanes] + spectra[1, 0, rows, lanes]
                        im = spectra[0, 1, rows, lanes] + spectra[1, 1, rows, lanes]
                        tiles.append(jnp.where(left_half, re, pltpu.roll(im, SPEC, 1)))
                        tiles.append(jnp.where(left_half, pltpu.roll(re, SPEC, 1), im))
                    tile = jnp.swapaxes(jnp.stack(tiles), 0, 1)
                    packed[pl.ds(w * 32 + g * 2, 2), o, q] = tile.reshape(2, 2, 16, LANES).astype(jnp.bfloat16)
                    return c

                lax.fori_loop(0, 16, turn, 0, unroll=True)

                @pl.when(w == 0)
                def _():
                    own_copy(o, q).start()

                others = peers(w, feed, time)

                @pl.when(w > 0)
                def _():
                    exchange(o, q, w * 32, others[0]).start()

                for i in range(1, 32):
                    exchange(o, q, w * 32 + i, others[i]).start()
                return carry

            lax.fori_loop(0, 4, section, 0)
            return carry

        lax.fori_loop(0, 2, parity, 0)
        return carry

    lax.fori_loop(0, 2, octet, 0)

    @pl.when(time < TIMES - 1)
    def _():
        halo_copy(0).wait_send()

    @pl.when((time == 0) | (time == 2))
    def _():
        halo_copy(1).wait_send()

    @pl.when(time == 1)
    def _():
        relay.wait_send()
        rest.wait_send()

    @pl.when(time == 3)
    def _():
        forward.wait_send()

    everything = pltpu.make_async_remote_copy(
        src_ref=packed.at[pl.ds(0, DEVICES - 1)], dst_ref=packed.at[pl.ds(0, DEVICES - 1)],
        send_sem=send_sem, recv_sem=recv_sem, device_id=(feed, time), device_id_type=MESH)
    everything.wait()
    own = packed.at[0]
    pltpu.make_async_copy(own, own, own_sem).wait()


def gather_spectra(voltages, pfb_taps, flags, coarse, fine):
    hbm = pl.BlockSpec(memory_space=pltpu.HBM)
    return pl.pallas_call(
        channelise,
        out_shape=jax.ShapeDtypeStruct((2, 2, TIMES, FEEDS, 2, 16, LANES), jnp.bfloat16),
        in_specs=[hbm, hbm, pl.BlockSpec(memory_space=pltpu.SMEM), hbm, hbm],
        out_specs=pl.BlockSpec(memory_space=pl.ANY),
        scratch_shapes=[
            pltpu.VMEM((2, OCT, SPEC * FRAME), jnp.int32),
            pltpu.VMEM((TAPS, FRAME), jnp.float32),
            pltpu.VMEM((2, DEVICES, HALF), jnp.float32),
            pltpu.VMEM((2, 2, 8, HALF), jnp.float32),
            pltpu.VMEM((2, 8, 16, FRAME), jnp.bfloat16),
            pltpu.VMEM((2, 8, 16, FRAME), jnp.bfloat16),
            pltpu.VMEM((2, 4, 2, 2, 128, HALF), jnp.bfloat16),
            pltpu.VMEM((2, 2, OCT, SPEC, HALF), jnp.bfloat16),
            pltpu.VMEM((2, 2, 128, OCT * SPEC), jnp.float32),
            pltpu.VMEM((DEVICES, 2, 2, 2, 16, LANES), jnp.bfloat16),
            pltpu.SemaphoreType.DMA((2, 2)),
            pltpu.SemaphoreType.DMA((3,)),
            pltpu.SemaphoreType.DMA((3,)),
            pltpu.SemaphoreType.DMA((3,)),
            pltpu.SemaphoreType.DMA,
            pltpu.SemaphoreType.DMA,
            pltpu.SemaphoreType.DMA,
        ],
        compiler_params=pltpu.CompilerParams(
            collective_id=0, has_side_effects=True, vmem_limit_bytes=48 << 20),
        name="channelise",
    )(voltages, pfb_taps, flags, coarse, fine)


def correlate(spec, out_hbm, left, right, result, out_sem):
    lane = lax.broadcasted_iota(jnp.int32, (1, LANES), 1)
    sign = jnp.where(lane < SPEC, 1.0, -1.0)
    dims = (((1,), (1,)), ((), ()))

    def put(step, j, c):
        q, p = step // 2, step % 2
        slot = step * 4 + j * 2 + c
        return pltpu.make_async_copy(result.at[slot], out_hbm.at[p, j, q, c], out_sem.at[slot])

    def channels(step, carry):
        q, p = step // 2, step % 2
        for j in range(2):
            for t in range(TIMES):
                tile = spec[q, p, t].astype(jnp.float32)
                tile = tile[:, :, j * OCT:(j + 1) * OCT, :].reshape(512, LANES)
                cols = slice(t * LANES, (t + 1) * LANES)
                right[j, :, cols] = tile.astype(jnp.bfloat16)
                left[j, :, cols] = (pltpu.roll(tile, SPEC, 1) * sign).astype(jnp.bfloat16)
            value = right[j]
            result[step * 4 + j * 2] = lax.dot_general(value, value, dims, preferred_element_type=jnp.float32)
            put(step, j, 0).start()
            result[step * 4 + j * 2 + 1] = lax.dot_general(left[j], value, dims, preferred_element_type=jnp.float32)
            put(step, j, 1).start()
        return carry

    lax.fori_loop(0, 4, channels, 0)
    for step in range(4):
        for j in range(2):
            for c in range(2):
                put(step, j, c).wait()


def visibilities(gathered):
    out = pl.pallas_call(
        correlate,
        out_shape=jax.ShapeDtypeStruct((2, 2, 2, 2, 512, 512), jnp.float32),
        in_specs=[pl.BlockSpec(memory_space=pltpu.VMEM)],
        out_specs=pl.BlockSpec(memory_space=pltpu.HBM),
        scratch_shapes=[
            pltpu.VMEM((2, 512, 512), jnp.bfloat16),
            pltpu.VMEM((2, 512, 512), jnp.bfloat16),
            pltpu.VMEM((16, 512, 512), jnp.float32),
            pltpu.SemaphoreType.DMA((16,)),
        ],
        compiler_params=pltpu.CompilerParams(vmem_limit_bytes=48 << 20),
        name="correlate",
    )(gathered)
    return out.reshape(8, 2, 512, 512)


def per_device(voltages, pfb_taps, feed_flags):
    coarse, fine = phase_tables()
    pinned = [
        pltpu.with_memory_space_constraint(x, pltpu.HBM)
        for x in (voltages, pfb_taps, feed_flags, jnp.asarray(coarse), jnp.asarray(fine))
    ]
    return visibilities(gather_spectra(*pinned))


def solution(mesh):
    return jax.shard_map(
        per_device,
        mesh=mesh,
        in_specs=(P("feed", "tm"), P(), P("feed")),
        out_specs=P(("feed", "tm"), None, None, None),
        check_vma=False,
    )
```

```python
import functools
import math

import jax
import jax.numpy as jnp
import numpy as np
from jax import lax
from jax.experimental import pallas as pl
from jax.experimental.pallas import tpu as pltpu
from jax.sharding import PartitionSpec as P

MESH = pl.DeviceIdType.MESH
LANES = 128
FRAME = 2048
HALF = FRAME // 2
TAPS = 16
FEEDS, TIMES = 32, 4
DEVICES = FEEDS * TIMES
SPEC = 64
OCT = 8
BLOCKS = SPEC // 16
DETOUR = 5


def peers(section, feed, time):
    core, y, x, z = time % 2, feed // 16 * 2 + time // 2, feed // 4 % 4, feed % 4
    cores = [lax.rem(core + i, 2) for i in range(2)]
    ys = [lax.rem(y + i, 4) for i in range(4)]
    ys = [(lax.div(v, 2) * 16, lax.rem(v, 2) * 2) for v in ys]
    xs = [lax.rem(x + i, 4) * 4 for i in range(4)]
    zs = [lax.rem(z + i + 3 * section, 4) for i in range(4)]
    found = []
    for i in range(32):
        offset = i * 47 % DEVICES
        y_feed, y_time = ys[offset // 2 % 4]
        found.append((y_feed + xs[offset // 8 % 4] + zs[offset // 32], y_time + cores[offset % 2]))
    return found


def phase_tables():
    n = np.arange(HALF)
    coarse = np.exp(-2j * np.pi * ((8 * np.arange(DEVICES)[:, None] * n) % FRAME) / FRAME)
    rows = np.tile(2 * np.arange(4), 2)[None, :, None] + np.arange(2)[:, None, None]
    scale = 1.0 / (128 * 16 * math.sqrt(FRAME))
    fine = scale * np.exp(-2j * np.pi * (rows * n % FRAME) / FRAME)
    coarse = np.stack([coarse.real, coarse.imag]).astype(np.float32)
    fine = np.stack([fine.real, fine.imag], axis=1).astype(np.float32)
    return coarse, fine


def fir(taps, x, first, last):
    sums = {}
    for m in range(first, last + 1):
        total = taps[0] * x[m]
        for p in range(1, len(taps)):
            total = total + taps[p] * x[m - p]
        sums[m] = total
    return sums


def fast_fir(taps, x):
    h0, h1 = taps[0::2], taps[1::2]
    x0 = {j // 2: v for j, v in x.items() if j % 2 == 0}
    x1 = {j // 2: v for j, v in x.items() if j % 2 == 1}
    both = {r: x0[r] + x1[r] for r in range(-7, 8)}
    even = fir(h0, x0, 0, 7)
    odd = fir(h1, x1, -1, 7)
    mixed = fir([a + b for a, b in zip(h0, h1)], both, 0, 7)
    sums = []
    for r in range(8):
        sums.append(even[r] + odd[r - 1])
        sums.append(mixed[r] - (even[r] + odd[r]))
    return sums


def channelise(
    volt_hbm, taps_hbm, flag_ref, coarse_hbm, fine_hbm, out_ref,
    volt, taps_ref, coarse_ref, fine_ref, edge, halo, table, folded, spectra, packed,
    in_sem, const_sem, halo_send, halo_recv, send_sem, recv_sem, own_sem,
):
    feed, time = lax.axis_index("feed"), lax.axis_index("tm")

    tail = (SPEC - 16) * FRAME
    edges, bodies = [], []
    for o in range(2):
        inputs = pl.ds(o * OCT, OCT)
        edges.append(pltpu.make_async_copy(
            volt_hbm.at[inputs, pl.ds(tail, 16 * FRAME)], volt.at[o, :, pl.ds(tail, 16 * FRAME)], in_sem.at[o, 0]))
        bodies.append(pltpu.make_async_copy(
            volt_hbm.at[inputs, pl.ds(0, tail)], volt.at[o, :, pl.ds(0, tail)], in_sem.at[o, 1]))
    fine_load = pltpu.make_async_copy(fine_hbm, fine_ref, const_sem.at[0])
    coarse_load = pltpu.make_async_copy(coarse_hbm, coarse_ref, const_sem.at[1])
    taps_load = pltpu.make_async_copy(taps_hbm, taps_ref, const_sem.at[2])
    for load in (*edges, fine_load, coarse_load, taps_load, *bodies):
        load.start()

    barrier = pltpu.get_barrier_semaphore()

    def greet(w, carry):
        others = peers(w, feed, time)

        @pl.when(w > 0)
        def _():
            pl.semaphore_signal(barrier, inc=1, device_id=others[0], device_id_type=MESH)

        for other in others[1:]:
            pl.semaphore_signal(barrier, inc=1, device_id=other, device_id_type=MESH)
        return carry

    lax.fori_loop(0, 4, greet, 0)

    upper = lax.broadcasted_iota(jnp.int32, (8, HALF), 0) < 4

    def make_table(q):
        fine_re, fine_im = fine_ref[q, 0], fine_ref[q, 1]

        def rows(w, carry):
            owners = [f * TIMES + t for f, t in peers(w, feed, time)]
            for group in range(8):
                parts = []
                for side in range(2):
                    two = owners[group * 4 + side * 2:group * 4 + side * 2 + 2]
                    phase = [[coarse_ref[c, pl.ds(d, 1), :] for c in range(2)] for d in two]
                    a_re, a_im = [jnp.where(upper, phase[0][c], phase[1][c]) for c in range(2)]
                    parts.append((a_re * fine_re - a_im * fine_im, a_re * fine_im + a_im * fine_re))
                for c in range(2):
                    value = jnp.concatenate([parts[0][c], parts[1][c]], axis=0)
                    high = value.astype(jnp.bfloat16)
                    low = (value - high.astype(jnp.float32)).astype(jnp.bfloat16)
                    table[q, w, 0, c, group * 16:(group + 1) * 16, :] = high
                    table[q, w, 1, c, group * 16:(group + 1) * 16, :] = low
            return carry

        lax.fori_loop(0, 4, rows, 0)

    def halo_copy(o):
        return pltpu.make_async_remote_copy(
            src_ref=edge.at[o], dst_ref=halo.at[o], send_sem=halo_send.at[o], recv_sem=halo_recv.at[o],
            device_id=(feed, lax.rem(time + 1, TIMES)), device_id_type=MESH)

    across = lax.rem(feed + FEEDS // 2, FEEDS)
    detour, straight = pl.ds(0, DETOUR), pl.ds(DETOUR, 8 - DETOUR)
    relay = pltpu.make_async_remote_copy(
        src_ref=edge.at[1, detour], dst_ref=edge.at[1, detour],
        send_sem=halo_send.at[2], recv_sem=halo_recv.at[2], device_id=(across, 3), device_id_type=MESH)
    forward = pltpu.make_async_remote_copy(
        src_ref=edge.at[1, detour], dst_ref=halo.at[1, detour],
        send_sem=halo_send.at[2], recv_sem=halo_recv.at[1], device_id=(across, 2), device_id_type=MESH)
    rest = pltpu.make_async_remote_copy(
        src_ref=edge.at[1, straight], dst_ref=halo.at[1, straight],
        send_sem=halo_send.at[1], recv_sem=halo_recv.at[1], device_id=(feed, 2), device_id_type=MESH)

    def pack_edge(o):
        def block(nb, carry):
            lanes = pl.ds(pl.multiple_of(nb * LANES, LANES), LANES)
            for pair in range(8):
                two = []
                for side in range(2):
                    at = pl.multiple_of(tail + (pair * 2 + side) * FRAME + nb * LANES, LANES)
                    two.append(volt[o, :, pl.ds(at, LANES)].astype(jnp.float32))
                edge[o, pair, :, lanes] = jnp.concatenate(two, axis=0).astype(jnp.bfloat16)
            return carry

        lax.fori_loop(0, FRAME // LANES, block, 0)

    edges[0].wait()

    @pl.when(time < TIMES - 1)
    def _():
        pack_edge(0)

    pl.semaphore_wait(barrier, DEVICES - 1)
    edges[1].wait()

    @pl.when(time < TIMES - 1)
    def _():
        halo_copy(0).start()
        pack_edge(1)

    @pl.when((time == 0) | (time == 2))
    def _():
        halo_copy(1).start()

    @pl.when(time == 1)
    def _():
        relay.start()

    fine_load.wait()
    coarse_load.wait()
    make_table(0)

    @pl.when(time == 0)
    def _():
        halo[...] = jnp.zeros_like(halo)

    taps_load.wait()
    sublane = lax.broadcasted_iota(jnp.int32, (OCT, LANES), 0)

    def flags_of(o):
        flag = jnp.zeros((OCT, LANES), jnp.float32)
        for i in range(OCT):
            flag = jnp.where(sublane == i, flag_ref[o * OCT + i].astype(jnp.float32), flag)
        return flag

    def filter_blocks(o, nb, flag, blocks):
        for mb in blocks:
            sides = []
            for side in range(2):
                lane0 = nb * LANES + side * HALF
                lanes = pl.ds(pl.multiple_of(lane0, LANES), LANES)
                taps = [jnp.broadcast_to(taps_ref[pl.ds(p, 1), lanes], (OCT, LANES)) for p in range(TAPS)]
                x = {}
                for j in range(-15, 16):
                    if mb == 0 and j < 0:
                        pair, odd = (16 + j) // 2, (16 + j) % 2
                        x[j] = halo[o, pair, :, lanes].astype(jnp.float32)[odd * OCT:(odd + 1) * OCT]
                    else:
                        at = pl.multiple_of((mb * 16 + j) * FRAME + lane0, LANES)
                        x[j] = volt[o, :, pl.ds(at, LANES)].astype(jnp.float32)
                sums = fast_fir(taps, x)
                value = jnp.swapaxes(jnp.stack([s * flag for s in sums]), 0, 1)
                sides.append(value.astype(jnp.bfloat16).astype(jnp.float32))
            rows = slice(mb * 16, (mb + 1) * 16)
            lanes = pl.ds(pl.multiple_of(nb * LANES, LANES), LANES)
            folded[o, 0, :, rows, lanes] = (sides[0] + sides[1]).astype(jnp.bfloat16)
            folded[o, 1, :, rows, lanes] = (sides[0] - sides[1]).astype(jnp.bfloat16)

    lane = lax.broadcasted_iota(jnp.int32, (8, LANES), 1)
    left_half = lane < SPEC

    def exchange(o, q, step, other):
        return pltpu.make_async_remote_copy(
            src_ref=packed.at[step, o, q], dst_ref=out_ref.at[q, pl.ds(0, 2), time, feed, o],
            send_sem=send_sem, recv_sem=recv_sem, device_id=other, device_id_type=MESH)

    def own_copy(o, q):
        return pltpu.make_async_copy(packed.at[0, o, q], out_ref.at[q, pl.ds(0, 2), time, feed, o], own_sem)

    def octet(o, carry):
        flag = flags_of(o)

        def later_blocks(nb, c):
            filter_blocks(o, nb, flag, range(1, BLOCKS))
            return c

        def first_block(nb, c):
            filter_blocks(o, nb, flag, range(1))
            return c

        pltpu.make_async_copy(
            volt_hbm.at[pl.ds(0, OCT), pl.ds(0, tail)], volt.at[o, :, pl.ds(0, tail)], in_sem.at[o, 1]).wait()
        lax.fori_loop(0, 8, later_blocks, 0)

        @pl.when((time == 1) & (o == 0))
        def _():
            rest.start()

        @pl.when((time == 3) & (o == 0))
        def _():
            relay.wait_recv()
            forward.start()

        @pl.when(time > 0)
        def _():
            halo_copy(o).wait_recv()

        lax.fori_loop(0, 8, first_block, 0)

        def parity(q, carry):
            @pl.when((o == 0) & (q == 1))
            def _():
                make_table(1)

            def section(w, carry):
                right = folded[o, q].reshape(OCT * SPEC, HALF)
                spectra[...] = lax.dot_general(
                    table[q, w].reshape(512, HALF), right, (((1,), (1,)), ((), ())),
                    preferred_element_type=jnp.float32).reshape(2, 2, 128, OCT * SPEC)

                def turn(g, c):
                    rows = pl.ds(pl.multiple_of(g * 8, 8), 8)
                    tiles = []
                    for pair in range(OCT // 2):
                        lanes = slice(pair * LANES, (pair + 1) * LANES)
                        re = spectra[0, 0, rows, lanes] + spectra[1, 0, rows, lanes]
                        im = spectra[0, 1, rows, lanes] + spectra[1, 1, rows, lanes]
                        tiles.append(jnp.where(left_half, re, pltpu.roll(im, SPEC, 1)))
                        tiles.append(jnp.where(left_half, pltpu.roll(re, SPEC, 1), im))
                    tile = jnp.swapaxes(jnp.stack(tiles), 0, 1)
                    packed[pl.ds(w * 32 + g * 2, 2), o, q] = tile.reshape(2, 2, 16, LANES).astype(jnp.bfloat16)
                    return c

                lax.fori_loop(0, 16, turn, 0, unroll=True)

                @pl.when(w == 0)
                def _():
                    own_copy(o, q).start()

                others = peers(w, feed, time)

                @pl.when(w > 0)
                def _():
                    exchange(o, q, w * 32, others[0]).start()

                for i in range(1, 32):
                    exchange(o, q, w * 32 + i, others[i]).start()
                return carry

            lax.fori_loop(0, 4, section, 0)
            return carry

        lax.fori_loop(0, 2, parity, 0)
        return carry

    lax.fori_loop(0, 2, octet, 0)

    @pl.when(time < TIMES - 1)
    def _():
        halo_copy(0).wait_send()

    @pl.when((time == 0) | (time == 2))
    def _():
        halo_copy(1).wait_send()

    @pl.when(time == 1)
    def _():
        relay.wait_send()
        rest.wait_send()

    @pl.when(time == 3)
    def _():
        forward.wait_send()

    everything = pltpu.make_async_remote_copy(
        src_ref=packed.at[pl.ds(0, DEVICES - 1)], dst_ref=packed.at[pl.ds(0, DEVICES - 1)],
        send_sem=send_sem, recv_sem=recv_sem, device_id=(feed, time), device_id_type=MESH)
    everything.wait()
    own = packed.at[0]
    pltpu.make_async_copy(own, own, own_sem).wait()


def gather_spectra(voltages, pfb_taps, flags, coarse, fine):
    hbm = pl.BlockSpec(memory_space=pltpu.HBM)
    return pl.pallas_call(
        channelise,
        out_shape=jax.ShapeDtypeStruct((2, 2, TIMES, FEEDS, 2, 16, LANES), jnp.bfloat16),
        in_specs=[hbm, hbm, pl.BlockSpec(memory_space=pltpu.SMEM), hbm, hbm],
        out_specs=pl.BlockSpec(memory_space=pl.ANY),
        scratch_shapes=[
            pltpu.VMEM((2, OCT, SPEC * FRAME), jnp.int32),
            pltpu.VMEM((TAPS, FRAME), jnp.float32),
            pltpu.VMEM((2, DEVICES, HALF), jnp.float32),
            pltpu.VMEM((2, 2, 8, HALF), jnp.float32),
            pltpu.VMEM((2, 8, 16, FRAME), jnp.bfloat16),
            pltpu.VMEM((2, 8, 16, FRAME), jnp.bfloat16),
            pltpu.VMEM((2, 4, 2, 2, 128, HALF), jnp.bfloat16),
            pltpu.VMEM((2, 2, OCT, SPEC, HALF), jnp.bfloat16),
            pltpu.VMEM((2, 2, 128, OCT * SPEC), jnp.float32),
            pltpu.VMEM((DEVICES, 2, 2, 2, 16, LANES), jnp.bfloat16),
            pltpu.SemaphoreType.DMA((2, 2)),
            pltpu.SemaphoreType.DMA((3,)),
            pltpu.SemaphoreType.DMA((3,)),
            pltpu.SemaphoreType.DMA((3,)),
            pltpu.SemaphoreType.DMA,
            pltpu.SemaphoreType.DMA,
            pltpu.SemaphoreType.DMA,
        ],
        compiler_params=pltpu.CompilerParams(
            collective_id=0, has_side_effects=True, vmem_limit_bytes=48 << 20),
        name="channelise",
    )(voltages, pfb_taps, flags, coarse, fine)


def correlate(spec, out_hbm, left, right, result, out_sem):
    lane = lax.broadcasted_iota(jnp.int32, (1, LANES), 1)
    sign = jnp.where(lane < SPEC, 1.0, -1.0)
    dims = (((1,), (1,)), ((), ()))

    def put(step, j, c):
        q, p = step // 2, step % 2
        slot = step * 4 + j * 2 + c
        return pltpu.make_async_copy(result.at[slot], out_hbm.at[p, j, q, c], out_sem.at[slot])

    def channels(step, carry):
        q, p = step // 2, step % 2
        for j in range(2):
            for t in range(TIMES):
                tile = spec[q, p, t].astype(jnp.float32)
                tile = tile[:, :, j * OCT:(j + 1) * OCT, :].reshape(512, LANES)
                cols = slice(t * LANES, (t + 1) * LANES)
                right[j, :, cols] = tile.astype(jnp.bfloat16)
                left[j, :, cols] = (pltpu.roll(tile, SPEC, 1) * sign).astype(jnp.bfloat16)
            value = right[j]
            result[step * 4 + j * 2] = lax.dot_general(value, value, dims, preferred_element_type=jnp.float32)
            put(step, j, 0).start()
            result[step * 4 + j * 2 + 1] = lax.dot_general(left[j], value, dims, preferred_element_type=jnp.float32)
            put(step, j, 1).start()
        return carry

    lax.fori_loop(0, 4, channels, 0)
    for step in range(4):
        for j in range(2):
            for c in range(2):
                put(step, j, c).wait()


def visibilities(gathered):
    out = pl.pallas_call(
        correlate,
        out_shape=jax.ShapeDtypeStruct((2, 2, 2, 2, 512, 512), jnp.float32),
        in_specs=[pl.BlockSpec(memory_space=pltpu.VMEM)],
        out_specs=pl.BlockSpec(memory_space=pltpu.HBM),
        scratch_shapes=[
            pltpu.VMEM((2, 512, 512), jnp.bfloat16),
            pltpu.VMEM((2, 512, 512), jnp.bfloat16),
            pltpu.VMEM((16, 512, 512), jnp.float32),
            pltpu.SemaphoreType.DMA((16,)),
        ],
        compiler_params=pltpu.CompilerParams(vmem_limit_bytes=48 << 20),
        name="correlate",
    )(gathered)
    return out.reshape(8, 2, 512, 512)


def per_device(voltages, pfb_taps, feed_flags):
    coarse, fine = phase_tables()
    pinned = [
        pltpu.with_memory_space_constraint(x, pltpu.HBM)
        for x in (voltages, pfb_taps, feed_flags, jnp.asarray(coarse), jnp.asarray(fine))
    ]
    return visibilities(gather_spectra(*pinned))


def solution(mesh):
    return jax.shard_map(
        per_device,
        mesh=mesh,
        in_specs=(P("feed", "tm"), P(), P("feed")),
        out_specs=P(("feed", "tm"), None, None, None),
        check_vma=False,
    )
```

```python
import functools
import math

import jax
import jax.numpy as jnp
import numpy as np
from jax import lax
from jax.experimental import pallas as pl
from jax.experimental.pallas import tpu as pltpu
from jax.sharding import PartitionSpec as P

MESH = pl.DeviceIdType.MESH
LANES = 128
FRAME = 2048
HALF = FRAME // 2
TAPS = 16
FEEDS, TIMES = 32, 4
DEVICES = FEEDS * TIMES
SPEC = 64
OCT = 8
BLOCKS = SPEC // 16
DETOUR = 5


def peers(section, feed, time):
    core, y, x, z = time % 2, feed // 16 * 2 + time // 2, feed // 4 % 4, feed % 4
    cores = [lax.rem(core + i, 2) for i in range(2)]
    ys = [lax.rem(y + i, 4) for i in range(4)]
    ys = [(lax.div(v, 2) * 16, lax.rem(v, 2) * 2) for v in ys]
    xs = [lax.rem(x + i, 4) * 4 for i in range(4)]
    zs = [lax.rem(z + i + 3 * section, 4) for i in range(4)]
    found = []
    for i in range(32):
        offset = i * 47 % DEVICES
        y_feed, y_time = ys[offset // 2 % 4]
        found.append((y_feed + xs[offset // 8 % 4] + zs[offset // 32], y_time + cores[offset % 2]))
    return found


def phase_tables():
    n = np.arange(HALF)
    coarse = np.exp(-2j * np.pi * ((8 * np.arange(DEVICES)[:, None] * n) % FRAME) / FRAME)
    rows = np.tile(2 * np.arange(4), 2)[None, :, None] + np.arange(2)[:, None, None]
    scale = 1.0 / (128 * 16 * math.sqrt(FRAME))
    fine = scale * np.exp(-2j * np.pi * (rows * n % FRAME) / FRAME)
    coarse = np.stack([coarse.real, coarse.imag]).astype(np.float32)
    fine = np.stack([fine.real, fine.imag], axis=1).astype(np.float32)
    return coarse, fine


def fir(taps, x, first, last):
    sums = {}
    for m in range(first, last + 1):
        total = taps[0] * x[m]
        for p in range(1, len(taps)):
            total = total + taps[p] * x[m - p]
        sums[m] = total
    return sums


def fast_fir(taps, x):
    h0, h1 = taps[0::2], taps[1::2]
    x0 = {j // 2: v for j, v in x.items() if j % 2 == 0}
    x1 = {j // 2: v for j, v in x.items() if j % 2 == 1}
    both = {r: x0[r] + x1[r] for r in range(-7, 8)}
    even = fir(h0, x0, 0, 7)
    odd = fir(h1, x1, -1, 7)
    mixed = fir([a + b for a, b in zip(h0, h1)], both, 0, 7)
    sums = []
    for r in range(8):
        sums.append(even[r] + odd[r - 1])
        sums.append(mixed[r] - (even[r] + odd[r]))
    return sums


def channelise(
    volt_hbm, taps_hbm, flag_ref, coarse_hbm, fine_hbm, out_ref,
    volt, taps_ref, coarse_ref, fine_ref, edge, halo, table, folded, spectra, packed,
    in_sem, const_sem, halo_send, halo_recv, send_sem, recv_sem, own_sem,
):
    feed, time = lax.axis_index("feed"), lax.axis_index("tm")

    tail = (SPEC - 16) * FRAME
    edges, bodies = [], []
    for o in range(2):
        inputs = pl.ds(o * OCT, OCT)
        edges.append(pltpu.make_async_copy(
            volt_hbm.at[inputs, pl.ds(tail, 16 * FRAME)], volt.at[o, :, pl.ds(tail, 16 * FRAME)], in_sem.at[o, 0]))
        bodies.append(pltpu.make_async_copy(
            volt_hbm.at[inputs, pl.ds(0, tail)], volt.at[o, :, pl.ds(0, tail)], in_sem.at[o, 1]))
    fine_load = pltpu.make_async_copy(fine_hbm, fine_ref, const_sem.at[0])
    coarse_load = pltpu.make_async_copy(coarse_hbm, coarse_ref, const_sem.at[1])
    taps_load = pltpu.make_async_copy(taps_hbm, taps_ref, const_sem.at[2])
    for load in (*edges, fine_load, coarse_load, taps_load, *bodies):
        load.start()

    barrier = pltpu.get_barrier_semaphore()

    def greet(w, carry):
        others = peers(w, feed, time)

        @pl.when(w > 0)
        def _():
            pl.semaphore_signal(barrier, inc=1, device_id=others[0], device_id_type=MESH)

        for other in others[1:]:
            pl.semaphore_signal(barrier, inc=1, device_id=other, device_id_type=MESH)
        return carry

    lax.fori_loop(0, 4, greet, 0)

    upper = lax.broadcasted_iota(jnp.int32, (8, HALF), 0) < 4

    def make_table(q):
        fine_re, fine_im = fine_ref[q, 0], fine_ref[q, 1]

        def rows(w, carry):
            owners = [f * TIMES + t for f, t in peers(w, feed, time)]
            for group in range(8):
                parts = []
                for side in range(2):
                    two = owners[group * 4 + side * 2:group * 4 + side * 2 + 2]
                    phase = [[coarse_ref[c, pl.ds(d, 1), :] for c in range(2)] for d in two]
                    a_re, a_im = [jnp.where(upper, phase[0][c], phase[1][c]) for c in range(2)]
                    parts.append((a_re * fine_re - a_im * fine_im, a_re * fine_im + a_im * fine_re))
                for c in range(2):
                    value = jnp.concatenate([parts[0][c], parts[1][c]], axis=0)
                    high = value.astype(jnp.bfloat16)
                    low = (value - high.astype(jnp.float32)).astype(jnp.bfloat16)
                    table[q, w, 0, c, group * 16:(group + 1) * 16, :] = high
                    table[q, w, 1, c, group * 16:(group + 1) * 16, :] = low
            return carry

        lax.fori_loop(0, 4, rows, 0)

    def halo_copy(o):
        return pltpu.make_async_remote_copy(
            src_ref=edge.at[o], dst_ref=halo.at[o], send_sem=halo_send.at[o], recv_sem=halo_recv.at[o],
            device_id=(feed, lax.rem(time + 1, TIMES)), device_id_type=MESH)

    across = lax.rem(feed + FEEDS // 2, FEEDS)
    detour, straight = pl.ds(0, DETOUR), pl.ds(DETOUR, 8 - DETOUR)
    relay = pltpu.make_async_remote_copy(
        src_ref=edge.at[1, detour], dst_ref=edge.at[1, detour],
        send_sem=halo_send.at[2], recv_sem=halo_recv.at[2], device_id=(across, 3), device_id_type=MESH)
    forward = pltpu.make_async_remote_copy(
        src_ref=edge.at[1, detour], dst_ref=halo.at[1, detour],
        send_sem=halo_send.at[2], recv_sem=halo_recv.at[1], device_id=(across, 2), device_id_type=MESH)
    rest = pltpu.make_async_remote_copy(
        src_ref=edge.at[1, straight], dst_ref=halo.at[1, straight],
        send_sem=halo_send.at[1], recv_sem=halo_recv.at[1], device_id=(feed, 2), device_id_type=MESH)

    def pack_edge(o):
        def block(nb, carry):
            lanes = pl.ds(pl.multiple_of(nb * LANES, LANES), LANES)
            for pair in range(8):
                two = []
                for side in range(2):
                    at = pl.multiple_of(tail + (pair * 2 + side) * FRAME + nb * LANES, LANES)
                    two.append(volt[o, :, pl.ds(at, LANES)].astype(jnp.float32))
                edge[o, pair, :, lanes] = jnp.concatenate(two, axis=0).astype(jnp.bfloat16)
            return carry

        lax.fori_loop(0, FRAME // LANES, block, 0)

    edges[0].wait()

    @pl.when(time < TIMES - 1)
    def _():
        pack_edge(0)

    fine_load.wait()
    coarse_load.wait()
    make_table(0)

    pl.semaphore_wait(barrier, DEVICES - 1)
    edges[1].wait()

    @pl.when(time < TIMES - 1)
    def _():
        halo_copy(0).start()
        pack_edge(1)

    @pl.when((time == 0) | (time == 2))
    def _():
        halo_copy(1).start()

    @pl.when(time == 1)
    def _():
        relay.start()

    @pl.when(time == 0)
    def _():
        halo[...] = jnp.zeros_like(halo)

    taps_load.wait()
    sublane = lax.broadcasted_iota(jnp.int32, (OCT, LANES), 0)

    def flags_of(o):
        flag = jnp.zeros((OCT, LANES), jnp.float32)
        for i in range(OCT):
            flag = jnp.where(sublane == i, flag_ref[o * OCT + i].astype(jnp.float32), flag)
        return flag

    def filter_blocks(o, nb, flag, blocks):
        for mb in blocks:
            sides = []
            for side in range(2):
                lane0 = nb * LANES + side * HALF
                lanes = pl.ds(pl.multiple_of(lane0, LANES), LANES)
                taps = [jnp.broadcast_to(taps_ref[pl.ds(p, 1), lanes], (OCT, LANES)) for p in range(TAPS)]
                x = {}
                for j in range(-15, 16):
                    if mb == 0 and j < 0:
                        pair, odd = (16 + j) // 2, (16 + j) % 2
                        x[j] = halo[o, pair, :, lanes].astype(jnp.float32)[odd * OCT:(odd + 1) * OCT]
                    else:
                        at = pl.multiple_of((mb * 16 + j) * FRAME + lane0, LANES)
                        x[j] = volt[o, :, pl.ds(at, LANES)].astype(jnp.float32)
                sums = fast_fir(taps, x)
                value = jnp.swapaxes(jnp.stack([s * flag for s in sums]), 0, 1)
                sides.append(value.astype(jnp.bfloat16).astype(jnp.float32))
            rows = slice(mb * 16, (mb + 1) * 16)
            lanes = pl.ds(pl.multiple_of(nb * LANES, LANES), LANES)
            folded[o, 0, :, rows, lanes] = (sides[0] + sides[1]).astype(jnp.bfloat16)
            folded[o, 1, :, rows, lanes] = (sides[0] - sides[1]).astype(jnp.bfloat16)

    lane = lax.broadcasted_iota(jnp.int32, (8, LANES), 1)
    left_half = lane < SPEC

    def exchange(o, q, step, other):
        return pltpu.make_async_remote_copy(
            src_ref=packed.at[step, o, q], dst_ref=out_ref.at[q, pl.ds(0, 2), time, feed, o],
            send_sem=send_sem, recv_sem=recv_sem, device_id=other, device_id_type=MESH)

    def own_copy(o, q):
        return pltpu.make_async_copy(packed.at[0, o, q], out_ref.at[q, pl.ds(0, 2), time, feed, o], own_sem)

    def octet(o, carry):
        flag = flags_of(o)

        def later_blocks(nb, c):
            filter_blocks(o, nb, flag, range(1, BLOCKS))
            return c

        def first_block(nb, c):
            filter_blocks(o, nb, flag, range(1))
            return c

        pltpu.make_async_copy(
            volt_hbm.at[pl.ds(0, OCT), pl.ds(0, tail)], volt.at[o, :, pl.ds(0, tail)], in_sem.at[o, 1]).wait()
        lax.fori_loop(0, 8, later_blocks, 0)

        @pl.when((time == 1) & (o == 0))
        def _():
            rest.start()

        @pl.when((time == 3) & (o == 0))
        def _():
            relay.wait_recv()
            forward.start()

        @pl.when(time > 0)
        def _():
            halo_copy(o).wait_recv()

        lax.fori_loop(0, 8, first_block, 0)

        def parity(q, carry):
            @pl.when((o == 0) & (q == 1))
            def _():
                make_table(1)

            def section(w, carry):
                right = folded[o, q].reshape(OCT * SPEC, HALF)
                spectra[...] = lax.dot_general(
                    table[q, w].reshape(512, HALF), right, (((1,), (1,)), ((), ())),
                    preferred_element_type=jnp.float32).reshape(2, 2, 128, OCT * SPEC)

                def turn(g, c):
                    rows = pl.ds(pl.multiple_of(g * 8, 8), 8)
                    tiles = []
                    for pair in range(OCT // 2):
                        lanes = slice(pair * LANES, (pair + 1) * LANES)
                        re = spectra[0, 0, rows, lanes] + spectra[1, 0, rows, lanes]
                        im = spectra[0, 1, rows, lanes] + spectra[1, 1, rows, lanes]
                        tiles.append(jnp.where(left_half, re, pltpu.roll(im, SPEC, 1)))
                        tiles.append(jnp.where(left_half, pltpu.roll(re, SPEC, 1), im))
                    tile = jnp.swapaxes(jnp.stack(tiles), 0, 1)
                    packed[pl.ds(w * 32 + g * 2, 2), o, q] = tile.reshape(2, 2, 16, LANES).astype(jnp.bfloat16)
                    return c

                lax.fori_loop(0, 16, turn, 0, unroll=True)

                @pl.when(w == 0)
                def _():
                    own_copy(o, q).start()

                others = peers(w, feed, time)

                @pl.when(w > 0)
                def _():
                    exchange(o, q, w * 32, others[0]).start()

                for i in range(1, 32):
                    exchange(o, q, w * 32 + i, others[i]).start()
                return carry

            lax.fori_loop(0, 4, section, 0)
            return carry

        lax.fori_loop(0, 2, parity, 0)
        return carry

    lax.fori_loop(0, 2, octet, 0)

    @pl.when(time < TIMES - 1)
    def _():
        halo_copy(0).wait_send()

    @pl.when((time == 0) | (time == 2))
    def _():
        halo_copy(1).wait_send()

    @pl.when(time == 1)
    def _():
        relay.wait_send()
        rest.wait_send()

    @pl.when(time == 3)
    def _():
        forward.wait_send()

    everything = pltpu.make_async_remote_copy(
        src_ref=packed.at[pl.ds(0, DEVICES - 1)], dst_ref=packed.at[pl.ds(0, DEVICES - 1)],
        send_sem=send_sem, recv_sem=recv_sem, device_id=(feed, time), device_id_type=MESH)
    everything.wait()
    own = packed.at[0]
    pltpu.make_async_copy(own, own, own_sem).wait()


def gather_spectra(voltages, pfb_taps, flags, coarse, fine):
    hbm = pl.BlockSpec(memory_space=pltpu.HBM)
    return pl.pallas_call(
        channelise,
        out_shape=jax.ShapeDtypeStruct((2, 2, TIMES, FEEDS, 2, 16, LANES), jnp.bfloat16),
        in_specs=[hbm, hbm, pl.BlockSpec(memory_space=pltpu.SMEM), hbm, hbm],
        out_specs=pl.BlockSpec(memory_space=pl.ANY),
        scratch_shapes=[
            pltpu.VMEM((2, OCT, SPEC * FRAME), jnp.int32),
            pltpu.VMEM((TAPS, FRAME), jnp.float32),
            pltpu.VMEM((2, DEVICES, HALF), jnp.float32),
            pltpu.VMEM((2, 2, 8, HALF), jnp.float32),
            pltpu.VMEM((2, 8, 16, FRAME), jnp.bfloat16),
            pltpu.VMEM((2, 8, 16, FRAME), jnp.bfloat16),
            pltpu.VMEM((2, 4, 2, 2, 128, HALF), jnp.bfloat16),
            pltpu.VMEM((2, 2, OCT, SPEC, HALF), jnp.bfloat16),
            pltpu.VMEM((2, 2, 128, OCT * SPEC), jnp.float32),
            pltpu.VMEM((DEVICES, 2, 2, 2, 16, LANES), jnp.bfloat16),
            pltpu.SemaphoreType.DMA((2, 2)),
            pltpu.SemaphoreType.DMA((3,)),
            pltpu.SemaphoreType.DMA((3,)),
            pltpu.SemaphoreType.DMA((3,)),
            pltpu.SemaphoreType.DMA,
            pltpu.SemaphoreType.DMA,
            pltpu.SemaphoreType.DMA,
        ],
        compiler_params=pltpu.CompilerParams(
            collective_id=0, has_side_effects=True, vmem_limit_bytes=48 << 20),
        name="channelise",
    )(voltages, pfb_taps, flags, coarse, fine)


def correlate(spec, out_hbm, left, right, result, out_sem):
    lane = lax.broadcasted_iota(jnp.int32, (1, LANES), 1)
    sign = jnp.where(lane < SPEC, 1.0, -1.0)
    dims = (((1,), (1,)), ((), ()))

    def put(step, j, c):
        q, p = step // 2, step % 2
        slot = step * 4 + j * 2 + c
        return pltpu.make_async_copy(result.at[slot], out_hbm.at[p, j, q, c], out_sem.at[slot])

    def channels(step, carry):
        q, p = step // 2, step % 2
        for j in range(2):
            for t in range(TIMES):
                tile = spec[q, p, t].astype(jnp.float32)
                tile = tile[:, :, j * OCT:(j + 1) * OCT, :].reshape(512, LANES)
                cols = slice(t * LANES, (t + 1) * LANES)
                right[j, :, cols] = tile.astype(jnp.bfloat16)
                left[j, :, cols] = (pltpu.roll(tile, SPEC, 1) * sign).astype(jnp.bfloat16)
            value = right[j]
            result[step * 4 + j * 2] = lax.dot_general(value, value, dims, preferred_element_type=jnp.float32)
            put(step, j, 0).start()
            result[step * 4 + j * 2 + 1] = lax.dot_general(left[j], value, dims, preferred_element_type=jnp.float32)
            put(step, j, 1).start()
        return carry

    lax.fori_loop(0, 4, channels, 0)
    for step in range(4):
        for j in range(2):
            for c in range(2):
                put(step, j, c).wait()


def visibilities(gathered):
    out = pl.pallas_call(
        correlate,
        out_shape=jax.ShapeDtypeStruct((2, 2, 2, 2, 512, 512), jnp.float32),
        in_specs=[pl.BlockSpec(memory_space=pltpu.VMEM)],
        out_specs=pl.BlockSpec(memory_space=pltpu.HBM),
        scratch_shapes=[
            pltpu.VMEM((2, 512, 512), jnp.bfloat16),
            pltpu.VMEM((2, 512, 512), jnp.bfloat16),
            pltpu.VMEM((16, 512, 512), jnp.float32),
            pltpu.SemaphoreType.DMA((16,)),
        ],
        compiler_params=pltpu.CompilerParams(vmem_limit_bytes=48 << 20),
        name="correlate",
    )(gathered)
    return out.reshape(8, 2, 512, 512)


def per_device(voltages, pfb_taps, feed_flags):
    coarse, fine = phase_tables()
    pinned = [
        pltpu.with_memory_space_constraint(x, pltpu.HBM)
        for x in (voltages, pfb_taps, feed_flags, jnp.asarray(coarse), jnp.asarray(fine))
    ]
    return visibilities(gather_spectra(*pinned))


def solution(mesh):
    return jax.shard_map(
        per_device,
        mesh=mesh,
        in_specs=(P("feed", "tm"), P(), P("feed")),
        out_specs=P(("feed", "tm"), None, None, None),
        check_vma=False,
    )
```
